1024 devices in a mesh: grid: 16 (over z), space: 32 (over x, y), spec: 2 (over core).
Axes of the slice: x: 4, y: 8, z: 16, core: 2. Of those that a mesh axis runs over, the one named last changes fastest.
Arguments:
- spectrum: float32 [16, 32, 36, 64, 128], P('grid', None, None, ('space', 'spec')), may hold values from 0.05 to 1
- land_sea: int32 [16, 64, 128], P('grid'), may hold values 0 or 1
- west_index: int32 [16, 64], P('grid'), may hold values from 0 to 63, each once within a row
- east_index: int32 [16, 64], P('grid'), may hold values from 0 to 63, each once within a row
- current_u: float32 [16, 64, 64, 128], P('grid', None, ('space', 'spec')), may hold values from -0.3 to 0.3
- current_v: float32 [16, 64, 64, 128], P('grid', None, ('space', 'spec')), may hold values from -0.3 to 0.3
- transfer: bfloat16 [1152, 1152], replicated, may hold values from -0.1875 to 0.1875
- wind_rate: float32 [36], replicated, may hold values from 0.1 to 1
- dissipation: float32 [36], replicated, may hold values from 0.5 to 4
Outputs:
- waves: float32 [16, 32, 36, 64, 128], P('grid', 'space', 'spec')
- stokes: float32 [16, 128, 64, 128], P('grid', None, ('space', 'spec'))
The draws below stay inside these ranges and needn't reach their ends.
Inputs may be any that keep to these rules, and one draw needn't show every extreme that they name: `land_sea`: 1 marks a sea cell, 0 a land cell. `west_index`: row g lists, for each row of grid g, the row of grid g - 1 whose easternmost cell borders it; each row of the array is a permutation of the 64 rows. `east_index`: row g lists, for each row of grid g, the row of grid g + 1 whose westernmost cell borders it; each row of the array is a permutation of the 64 rows.
All inputs are finite; a program needn't handle non-finite values. No bound on the sum of `land_sea` on one device may be relied on, other than what follows from the above.
Results may differ from the reference program's by a relative error of at most 0.00082.
Values sent between devices are 32-bit elements; how exact they have to be, the bound alone decides.
No kernel may reach another device: no remote copies, remote signals or barrier semaphores. Data moves between devices by JAX's collectives and lax.ppermute only.
A program may use at most 64 MiB of HBM per device.

```python
import math
import jax
import jax.numpy as jnp
from jax import lax

ND = 32
NF = 36
LEV = 64
NCOL = 128
SUBSTEPS = 1
NGRID = 16
NROW = 64
COMPS = 1152


def place_ends(drawn, rng, least, largest):
    dims = drawn.shape
    spot = [jax.random.randint(jax.random.fold_in(rng, axis), (), 0, dims[axis]) for axis in range(len(dims))]
    drawn = drawn.at[tuple(spot)].set(least)
    longest = dims.index(max(dims))
    spot[longest] = (spot[longest] + 1) % dims[longest]
    return drawn.at[tuple(spot)].set(largest)


def block_scale(stream_key, extent, shards, least, top_value):
    level = 1.0
    for axis_at, shards_of in shards:
        heights = jax.random.uniform(jax.random.fold_in(jax.random.fold_in(stream_key, 6), axis_at), (shards_of,), jnp.float32, least / len(shards), top_value / len(shards))
        level = level * jnp.repeat(jnp.exp(heights), extent[axis_at] // shards_of).reshape((-1,) + (1,) * (len(extent) - 1 - axis_at))
    return level


def bell_draw(own_key, extent, spread, reach, held_as=jnp.bfloat16):
    result = jax.random.normal(own_key, extent, jnp.float32) * spread
    return jnp.minimum(jnp.maximum(result, -reach), reach).astype(held_as)


def setup_inputs(seed: int = 0) -> dict:
    keys = jax.random.split(jax.random.key(seed), 10)
    return {
        "spectrum": jnp.clip(jnp.exp(math.log(1.0) - 2.9957323 * jax.random.uniform(keys[0], (NGRID, ND, NF, NROW, NCOL), jnp.float32) ** block_scale(keys[0], (NGRID, ND, NF, NROW, NCOL), ((0, 16), (3, 64)), -0.2, 0.2)), 0.05, 1.0),
        "land_sea": place_ends((jax.random.randint(keys[1], (NGRID, NROW, NCOL), 0, 5) < 4).astype(jnp.int32), jax.random.fold_in(keys[1], 1), 0, 1),
        "west_index": jax.vmap(lambda own: jax.random.permutation(own, NROW))(jax.random.split(keys[2], NGRID)).reshape((NGRID, NROW)).astype(jnp.int32),
        "east_index": jax.vmap(lambda own: jax.random.permutation(own, NROW))(jax.random.split(keys[3], NGRID)).reshape((NGRID, NROW)).astype(jnp.int32),
        "current_u": jnp.clip(jax.random.uniform(keys[4], (NGRID, LEV, NROW, NCOL), jnp.float32, -0.3, 0.3) * block_scale(keys[4], (NGRID, LEV, NROW, NCOL), ((0, 16), (2, 64)), -0.4, 0.0), -0.3, 0.3),
        "current_v": jnp.clip(jax.random.uniform(keys[5], (NGRID, LEV, NROW, NCOL), jnp.float32, -0.3, 0.3) * block_scale(keys[5], (NGRID, LEV, NROW, NCOL), ((0, 16), (2, 64)), -0.4, 0.0), -0.3, 0.3),
        "transfer": bell_draw(keys[6], (COMPS, COMPS), COMPS ** -0.5, 0.1875),
        "wind_rate": jnp.clip(jnp.exp(jax.random.uniform(keys[7], (NF,), jnp.float32, math.log(0.1), math.log(1.0))), 0.1, 1.0),
        "dissipation": jnp.clip(jnp.exp(jax.random.uniform(keys[8], (NF,), jnp.float32, math.log(0.5), math.log(4.0))), 0.5, 4.0),
    }


sigma_base = 0.2199
gravity = 9.81
growth = 1.1
courant_scale = 3.0
time_step = 0.5
stokes_gain = 2.0
highest = lax.Precision.HIGHEST

def tables(freq_count, directions, levels):
    freq_steps = jnp.arange(freq_count).astype(jnp.float32)
    radian_freq = sigma_base * growth ** freq_steps
    wavenum = radian_freq * radian_freq / gravity
    speeds = courant_scale * growth ** (-freq_steps)
    angles = 2.0 * jnp.pi * jnp.arange(directions).astype(jnp.float32) / directions
    depths = -(jnp.arange(levels).astype(jnp.float32) + 0.5)
    decays = jnp.exp(2.0 * wavenum[:, None] * depths[None, :])
    current_weight = decays / lax.optimization_barrier(jnp.sum(decays, axis=1, keepdims=True))
    drifts = (radian_freq * wavenum)[:, None] * decays
    drifts = drifts / lax.optimization_barrier(jnp.sum(drifts, axis=0, keepdims=True))
    return (speeds, angles, current_weight, drifts)

def sweep_matrix(courant, length):
    forward = jnp.maximum(courant, 0.0)[..., None, None]
    backward = jnp.maximum(-courant, 0.0)[..., None, None]
    places = jnp.arange(length)
    offset = (places[:, None] - places[None, :]).astype(courant.dtype)
    lower_part = jnp.where(offset >= 0, (forward / (1.0 + forward)) ** jnp.maximum(offset, 0.0) / (1.0 + forward), 0.0)
    upper_part = jnp.where(offset <= 0, (backward / (1.0 + backward)) ** jnp.maximum(-offset, 0.0) / (1.0 + backward), 0.0)
    return lower_part + upper_part - jnp.eye(length, dtype=courant.dtype)

def sources(spectra, sea_points, transfer, wind_gain, damping):
    for substep in range(SUBSTEPS):
        rounded = spectra.astype(jnp.bfloat16)
        redist = jnp.dot(transfer, rounded, preferred_element_type=jnp.float32)
        energy = lax.optimization_barrier(jnp.mean(spectra * spectra, axis=0, keepdims=True))
        spectra = sea_points * (spectra * (1.0 + time_step * wind_gain) + time_step * redist) / (1.0 + time_step * damping * energy)
    return spectra

def propagate(wave_field, ghost_west, ghost_east, flow_field, sea_cells, sweep_cols, sweep_rows, courant_x):
    flow_x = flow_field[0][None]
    flow_y = flow_field[1][None]
    west_cells = jnp.concatenate([ghost_west[..., None], wave_field[..., :-1]], axis=-1)
    east_cells = jnp.concatenate([wave_field[..., 1:], ghost_east[..., None]], axis=-1)
    blank_row = jnp.zeros_like(wave_field[..., :1, :])
    north_cells = jnp.concatenate([blank_row, wave_field[..., :-1, :]], axis=-2)
    south_cells = jnp.concatenate([wave_field[..., 1:, :], blank_row], axis=-2)
    moved = wave_field - jnp.maximum(flow_x, 0.0) * (wave_field - west_cells) - jnp.maximum(-flow_x, 0.0) * (wave_field - east_cells) - jnp.maximum(flow_y, 0.0) * (wave_field - north_cells) - jnp.maximum(-flow_y, 0.0) * (wave_field - south_cells)
    inflow_west = jnp.maximum(courant_x, 0.0)[..., None] * ghost_west
    inflow_east = jnp.maximum(-courant_x, 0.0)[..., None] * ghost_east
    moved = moved.at[..., 0].add(inflow_west).at[..., -1].add(inflow_east)
    swept = jnp.einsum('abij,abyj->abyi', sweep_cols, moved, precision=highest)
    swept = jnp.einsum('abij,abjx->abix', sweep_rows, swept, precision=highest)
    return sea_cells * swept

def ghosts(wave_all, west_index, east_index):
    east_cols = wave_all[..., -1]
    west_cols = wave_all[..., 0]
    from_left = jnp.concatenate([jnp.zeros_like(east_cols[:1]), east_cols[:-1]], axis=0)
    from_right = jnp.concatenate([west_cols[1:], jnp.zeros_like(west_cols[:1])], axis=0)
    pick_west = jnp.broadcast_to(west_index[:, None, None, :], from_left.shape)
    pick_east = jnp.broadcast_to(east_index[:, None, None, :], from_right.shape)
    return (jnp.take_along_axis(from_left, pick_west, axis=3), jnp.take_along_axis(from_right, pick_east, axis=3))

def reference(spectrum, land_sea, west_index, east_index, current_u, current_v, transfer, wind_rate, dissipation):
    speeds, angles, current_weight, drifts = tables(NF, ND, LEV)
    courant_x = speeds[None, :] * jnp.cos(angles)[:, None]
    courant_y = speeds[None, :] * jnp.sin(angles)[:, None]
    sweep_cols = sweep_matrix(courant_x, NCOL)
    sweep_rows = sweep_matrix(courant_y, NROW)
    wind_gain = (0.5 * (1.0 + jnp.cos(angles))[:, None] * wind_rate[None, :]).reshape(COMPS, 1)
    damping = jnp.broadcast_to(dissipation[None, :], (ND, NF)).reshape(COMPS, 1)
    drift_x = drifts.T[:, None, :] * (jnp.cos(angles) * stokes_gain / math.sqrt(ND))[None, :, None]
    drift_y = drifts.T[:, None, :] * (jnp.sin(angles) * stokes_gain / math.sqrt(ND))[None, :, None]
    stokes_table = jnp.concatenate([drift_x, drift_y], 0).reshape(2 * LEV, COMPS)
    sea_all = land_sea.astype(jnp.float32)
    flow_all = jnp.stack([jnp.einsum('fl,glyx->gfyx', current_weight, current_u, precision=highest), jnp.einsum('fl,glyx->gfyx', current_weight, current_v, precision=highest)], axis=1)

    def first_sources(grid_pair):
        wave_grid, sea_grid = grid_pair
        updated = sources(wave_grid.reshape(COMPS, NROW * NCOL), sea_grid.reshape(1, NROW * NCOL), transfer, wind_gain, damping)
        return updated.reshape(ND, NF, NROW, NCOL)

    def second_sources(grid_pair):
        wave_grid, sea_grid = grid_pair
        updated = sources(wave_grid.reshape(COMPS, NROW * NCOL), sea_grid.reshape(1, NROW * NCOL), transfer, wind_gain, damping)
        drift_grid = jnp.dot(stokes_table, updated, precision=highest)
        return (updated.reshape(ND, NF, NROW, NCOL), drift_grid.reshape(2 * LEV, NROW, NCOL))

    def propagate_grid(grid_args):
        wave_grid, ghost_west, ghost_east, flow_grid, sea_grid = grid_args
        return propagate(wave_grid, ghost_west, ghost_east, flow_grid, sea_grid, sweep_cols, sweep_rows, courant_x)
    after_sources = lax.map(first_sources, (spectrum, sea_all))
    ghost_west, ghost_east = ghosts(after_sources, west_index, east_index)
    after_first = lax.map(propagate_grid, (after_sources, ghost_west, ghost_east, flow_all, sea_all))
    after_second, stokes = lax.map(second_sources, (after_first, sea_all))
    ghost_west, ghost_east = ghosts(after_second, west_index, east_index)
    waves = lax.map(propagate_grid, (after_second, ghost_west, ghost_east, flow_all, sea_all))
    return (waves, stokes)
```

```python
import jax
import jax.numpy as jnp
import numpy as np
from jax import lax
from jax.experimental import pallas as pl
from jax.experimental.pallas import tpu as pltpu
from jax.sharding import PartitionSpec as P

ND, NF, LEV, NCOL, NROW = 32, 36, 64, 128, 64
COMPS = ND * NF
TILES = COMPS // 128
PLANE = ("space", "spec")
EVERY = ("grid", "space", "spec")
f32 = np.float32
highest = lax.Precision.HIGHEST
MSG = 20
VM = pl.BlockSpec(memory_space=pltpu.VMEM)
SM = pl.BlockSpec(memory_space=pltpu.SMEM)
INTERPRET = False


def host_tables():
    steps = np.arange(NF).astype(f32)
    radian = f32(0.2199) * f32(1.1) ** steps
    wave = radian * radian / f32(9.81)
    speeds = f32(3.0) * f32(1.1) ** (-steps)
    angles = f32(2.0 * np.pi) * np.arange(ND).astype(f32) / f32(ND)
    depths = -(np.arange(LEV).astype(f32) + f32(0.5))
    decays = np.exp(2.0 * wave[:, None].astype(np.float64) * depths[None, :])
    current = decays / decays.sum(1, keepdims=True)
    drifts = (radian * wave)[:, None] * decays
    drifts = drifts / drifts.sum(0, keepdims=True)
    cosines, sines = np.cos(angles), np.sin(angles)
    return speeds, cosines, sines, current, drifts


SPEEDS, COS, SIN, CURRENT, DRIFTS = host_tables()
CX = (COS[:, None] * SPEEDS[None, :]).astype(f32).reshape(-1)
CY = (SIN[:, None] * SPEEDS[None, :]).astype(f32).reshape(-1)


def scan_table(courant, block, extra):
    rows = []
    for part in (np.maximum(courant, 0), np.maximum(-courant, 0)):
        part = part.astype(np.float64)
        ratio = part / (1.0 + part)
        rows.append(1.0 / (1.0 + part))
        rows.extend(ratio**n for n in range(1, block + 1))
        rows.extend(ratio ** (block * n) for n in extra)
    rows.append(np.maximum(courant, 0))
    rows.append(np.maximum(-courant, 0))
    return np.stack(rows).astype(f32)


KX = scan_table(CX, 16, (2, 4))
KY = scan_table(CY, 8, (2, 4))
KY[-2:] = KX[-2:]
INFLOW = (KX.shape[0] - 2, KY.shape[0] - 2)
HAS = {
    name: [[bool((s * c[128 * k : 128 * k + 128] > 0).any()) for s in (1, -1)] for k in range(TILES)]
    for name, c in (("x", CX), ("y", CY))
}
FLOW_W = np.zeros((128, 2 * COMPS), f32)
FLOW_W[:LEV, :COMPS] = np.tile(CURRENT.T, (1, ND))
FLOW_W[LEV:, COMPS:] = np.tile(CURRENT.T, (1, ND))
GAIN = 2.0 / np.sqrt(float(ND))
STOKES_T = np.concatenate(
    [(DRIFTS.T[:, None, :] * (trig * GAIN)[None, :, None]).reshape(LEV, COMPS) for trig in (COS, SIN)]
).T.astype(f32)


def sweep_scalars():
    c = np.abs(CX.astype(np.float64)).reshape(ND, NF)
    ratio = c / (1 + c)
    cols = [1 / (1 + c), ratio] + [ratio**n for n in (2, 16, 32, 64)]
    cols += [np.zeros_like(c)] * 2
    table = np.stack(cols, -1).reshape(ND * 2, NF // 2, 8)
    return table.reshape(ND * 2, -1).astype(f32)


SWEEP = sweep_scalars()
AHEAD = (COS >= 0).astype(np.int32)


def down(x, first=None):
    top = jnp.zeros_like(x[:1]) if first is None else first
    return jnp.concatenate([top, x[:-1]], axis=0)


def up(x, last=None):
    end = jnp.zeros_like(x[:1]) if last is None else last
    return jnp.concatenate([x[1:], end], axis=0)


def hop(x, n, forward):
    z = jnp.zeros_like(x[:n])
    return jnp.concatenate([z, x[:-n]] if forward else [x[n:], z], axis=0)


def block_scan(tiles, table, base, lanes, forward):
    block = len(tiles)
    row = lambda n: table[pl.ds(base + n, 1), lanes]
    scale, ratio = row(0), row(1)
    order = list(range(block)) if forward else list(range(block - 1, -1, -1))
    out = [None] * block
    state = None
    for t in order:
        state = scale * tiles[t] if state is None else scale * tiles[t] + ratio * state
        out[t] = state
    ends = state
    ends = ends + row(block) * hop(ends, 1, forward)
    ends = ends + row(block + 1) * hop(ends, 2, forward)
    ends = ends + row(block + 2) * hop(ends, 4, forward)
    carry = hop(ends, 1, forward)
    for n, t in enumerate(order):
        out[t] = out[t] + row(n + 1) * carry
    return out


def sweep(tiles, table, k, has):
    lanes = pl.ds(128 * k, 128)
    size = len(tiles) + 3
    if has[0]:
        tiles = block_scan(tiles, table, 0, lanes, True)
    if has[1]:
        tiles = block_scan(tiles, table, size, lanes, False)
    return tiles


def source_step(spec_ref, transfer, wind, damp, sea_row, out_ref):
    spectra = spec_ref[...]
    redist = jnp.dot(transfer[...], spectra.astype(jnp.bfloat16), preferred_element_type=jnp.float32)
    energy = jnp.sum(spectra * spectra, axis=0, keepdims=True) * (1.0 / COMPS)
    turns = lax.broadcasted_iota(jnp.int32, (2 * NF, NF), 0)
    turns = jnp.where(turns >= NF, turns - NF, turns)
    pick = turns == lax.broadcasted_iota(jnp.int32, (2 * NF, NF), 1)
    wind_col = jnp.sum(jnp.where(pick, wind, 0.0), axis=1, keepdims=True)
    damp_col = jnp.sum(jnp.where(pick, damp, 0.0), axis=1, keepdims=True)
    shrink = sea_row / (1.0 + 0.5 * damp_col * energy)
    first = lax.broadcasted_iota(jnp.int32, (2 * NF, 1), 0) < NF
    for pair in range(ND // 2):
        rows = slice(2 * NF * pair, 2 * NF * (pair + 1))
        near, far = (float(0.25 * (1.0 + COS[2 * pair + n])) for n in range(2))
        gain = 1.0 + jnp.where(first, near, far) * wind_col
        out_ref[rows, :] = (spectra[rows] * gain + 0.5 * redist[rows]) * shrink


def rows_source(place, spec, transfer, wind, damp, land_sea, out, east, west, work):
    sea_row = land_sea[pl.ds(place[0], 1), :].astype(jnp.float32)
    source_step(spec, transfer, wind[...], damp[...], sea_row, work)
    for k in range(TILES):
        turned = work[128 * k : 128 * k + 128, :].T
        out[pl.ds(k, 128, stride=TILES), :] = turned
        west[pl.ds(k, 1), :] = turned[:1]
        east[pl.ds(k, 1), :] = turned[127:]


def flows(uv, weights, east_flow, north_flow):
    for k in range(TILES):
        for n, ref in ((0, east_flow), (TILES, north_flow)):
            lanes = slice(128 * (k + n), 128 * (k + n) + 128)
            ref[k] = jnp.dot(uv, weights[:, lanes], precision=highest, preferred_element_type=jnp.float32)


def rows_flow(u, v, weights, uv, east_flow, north_flow):
    turned = jnp.concatenate([u[...], v[...]], axis=0).T
    uv[...] = turned
    flows(turned, weights, east_flow, north_flow)


def advect(mid, west, east, north, south, a, b):
    return (
        mid
        - jnp.maximum(a, 0.0) * (mid - west)
        - jnp.maximum(-a, 0.0) * (mid - east)
        - jnp.maximum(b, 0.0) * (mid - north)
        - jnp.maximum(-b, 0.0) * (mid - south)
    )


def rows_move(place, spec, north, south, ghosts, east_flow, north_flow, uv, table, out):
    west_at, east_at = place[1], place[2]
    edge = lax.broadcasted_iota(jnp.int32, (8, 128), 0)
    for k in range(TILES):
        tile = lambda ref, t: ref[pl.ds(t * TILES + k, 8, stride=16 * TILES), :]
        flow = lambda ref, t: ref.at[k][pl.ds(t, 8, stride=16), :]
        ghost_west = ghosts[pl.ds(west_at * (2 * TILES) + k, 1), :]
        ghost_east = ghosts[pl.ds(east_at * (2 * TILES) + TILES + k, 1), :]
        mids = [tile(spec, t) for t in range(16)]
        moved = []
        for t in range(16):
            west = mids[t - 1] if t else down(mids[15], ghost_west)
            east = mids[t + 1] if t < 15 else up(mids[0], ghost_east)
            moved.append(
                advect(mids[t], west, east, tile(north, t), tile(south, t), flow(east_flow, t), flow(north_flow, t))
            )
        lanes = pl.ds(128 * k, 128)
        into_west = table[pl.ds(INFLOW[0], 1), lanes] * ghost_west
        into_east = table[pl.ds(INFLOW[0] + 1, 1), lanes] * ghost_east
        moved[0] = moved[0] + jnp.where(edge == 0, into_west, 0.0)
        moved[15] = moved[15] + jnp.where(edge == 7, into_east, 0.0)
        for t, value in enumerate(sweep(moved, table, k, HAS["x"][k])):
            out[pl.ds(t * (TILES + 1) + k, 8, stride=16 * (TILES + 1)), :] = value
    out[pl.ds(TILES, 128, stride=TILES + 1), :] = uv[...]


def columns_source(place, arrived, transfer, wind, damp, land_sea, table, near, far, sea, turned, held, work):
    lane = lax.broadcasted_iota(jnp.int32, (NROW, NCOL), 1)
    land = land_sea[...].astype(jnp.float32)
    for side in range(2):
        column = jnp.sum(jnp.where(lane == 2 * place[0] + side, land, 0.0), axis=1, keepdims=True)
        sea[NROW * side : NROW * (side + 1), :] = jnp.broadcast_to(column, (NROW, 128))
    for k in range(TILES):
        for side in range(2):
            tiles = [
                arrived[pl.ds((2 * s + side) * (TILES + 1) + k, 8, stride=16 * (TILES + 1)), :] for s in range(8)
            ]
            for s, value in enumerate(sweep(tiles, table, k, HAS["y"][k])):
                at = pl.ds(NROW * side + s, 8, stride=8)
                turned.at[k][at, :] = value * sea[at, :]
        held[128 * k : 128 * k + 128, :] = turned[k].T
    source_step(held, transfer, wind[...], damp[...], sea[...].T[:1], work)
    for k in range(TILES):
        back = work[128 * k : 128 * k + 128, :].T
        near[k] = back[:NROW]
        far[k] = back[NROW:]


def columns_flow(arrived, near, far, weights, stokes_table, east_flow, north_flow, stokes):
    uv = jnp.concatenate(
        [arrived[pl.ds(TILES + side * (TILES + 1), NROW, stride=MSG), :] for side in range(2)], axis=0
    )
    flows(uv, weights, east_flow, north_flow)
    total = jnp.zeros((128, 128), jnp.float32)
    for k in range(TILES):
        spectra = jnp.concatenate([near[k], far[k]], axis=0)
        total = total + jnp.dot(
            spectra, stokes_table[128 * k : 128 * k + 128, :], precision=highest, preferred_element_type=jnp.float32
        )
    stokes[...] = total


def columns_move(
    flags, near, far, from_west, from_east, pick_west, pick_east, east_flow, north_flow, stokes, table, out,
    west_halo, east_halo, held, turned,
):
    for k in range(TILES):
        west_halo[...] = jnp.dot(pick_west[...], from_west[k], precision=highest, preferred_element_type=jnp.float32)
        east_halo[...] = jnp.dot(pick_east[...], from_east[k], precision=highest, preferred_element_type=jnp.float32)
        lanes = pl.ds(128 * k, 128)
        into = [table[pl.ds(INFLOW[1] + n, 1), lanes] * flags[n] for n in range(2)]
        cells = [[ref.at[k][pl.ds(s, 8, stride=8), :] for s in range(8)] for ref in (near, far)]
        for side in range(2):
            halo = west_halo if side == 0 else east_halo
            moved = []
            for s in range(8):
                at = pl.ds(NROW * side + s, 8, stride=8)
                beyond = halo[pl.ds(s, 8, stride=8), :]
                mids = cells[side]
                north = mids[s - 1] if s else down(mids[7])
                south = mids[s + 1] if s < 7 else up(mids[0])
                west = beyond if side == 0 else cells[0][s]
                east = cells[1][s] if side == 0 else beyond
                value = advect(mids[s], west, east, north, south, east_flow.at[k][at, :], north_flow.at[k][at, :])
                moved.append(value + into[side] * beyond)
            for s, value in enumerate(sweep(moved, table, k, HAS["y"][k])):
                held[pl.ds(NROW * side + s, 8, stride=8), :] = value
        turned[128 * k : 128 * k + 128, :] = held[...].T
    half = NF // 2
    for i in range(half):
        out[pl.ds(i, 64, stride=MSG), :] = turned[pl.ds(i, 64, stride=half), :]
    for side in range(2):
        out[pl.ds(half + side, 64, stride=MSG), :] = stokes[NROW * side : NROW * (side + 1), :]


def comps_sweep(ahead, scalars, arrived, land_sea, waves, stokes, work, rows):
    half = NF // 2
    low = lax.broadcasted_iota(jnp.int32, (8, 128), 1) < NROW

    def solve(forward):
        for i in range(half):
            scale, ratio, ratio2, hop1, hop2, hop4 = (scalars[0, 8 * i + n] for n in range(6))
            tiles = [arrived[pl.ds(t * MSG + i, 8, stride=8 * MSG), :] * scale for t in range(8)]
            order = list(range(8)) if forward else list(range(7, -1, -1))
            state, states = None, {}
            for t in order:
                swapped = pltpu.roll(tiles[t], NROW, 1)
                a = tiles[t] + ratio * swapped
                b = swapped + ratio * tiles[t]
                pair = jnp.where(low, b, a) if forward else jnp.where(low, a, b)
                state = pair if state is None else pair + ratio2 * state
                states[t] = state
            ends = state
            ends = ends + hop1 * hop(ends, 1, forward)
            ends = ends + hop2 * hop(ends, 2, forward)
            ends = ends + hop4 * hop(ends, 4, forward)
            before = hop(ends, 1, forward)
            carry = before
            for t in order:
                carry = ratio2 * carry
                now = states[t] + carry
                other = tiles[t] + ratio * before
                value = jnp.where(low, other, now) if forward else jnp.where(low, now, other)
                work[pl.ds(NROW * i + t, 8, stride=8), :] = value
                before = now

    @pl.when(ahead[0] == 1)
    def _():
        solve(True)

    @pl.when(ahead[0] == 0)
    def _():
        solve(False)

    land = land_sea[...].astype(jnp.float32)
    which = lax.broadcasted_iota(jnp.int32, (128, 256), 0)
    there = lax.broadcasted_iota(jnp.int32, (128, 256), 1)
    spread = [
        (2 * jnp.where(which >= NROW, which - NROW, which) + side + jnp.where(which >= NROW, 128, 0) == there)
        .astype(jnp.float32)
        .astype(jnp.bfloat16)
        for side in range(2)
    ]
    for pair in range(half // 2):
        both = work[128 * pair : 128 * pair + 128, :].T
        total = jnp.zeros((NROW, 256), jnp.float32)
        for side in range(2):
            left = both[NROW * side : NROW * (side + 1)]
            for n in range(3):
                part = left.astype(jnp.bfloat16)
                total = total + jnp.dot(part, spread[side], preferred_element_type=jnp.float32)
                if n < 2:
                    left = left - part.astype(jnp.float32)
        for n in range(2):
            i = 2 * pair + n
            waves[NROW * i : NROW * (i + 1), :] = total[:, 128 * n : 128 * n + 128] * land
    for side in range(2):
        rows[pl.ds(side, 64, stride=2), :] = arrived[pl.ds(half + side, 64, stride=MSG), :]
    stokes[...] = rows[...].T


def kernel(body, outs, scratch, specs, flops, nbytes, name):
    return pl.pallas_call(
        body,
        out_shape=[jax.ShapeDtypeStruct(s, jnp.float32) for s in outs],
        in_specs=specs,
        out_specs=[VM] * len(outs),
        scratch_shapes=[pltpu.VMEM(s, jnp.float32) for s in scratch],
        compiler_params=pltpu.CompilerParams(vmem_limit_bytes=32 << 20),
        cost_estimate=pl.CostEstimate(flops=flops, bytes_accessed=nbytes, transcendentals=0),
        interpret=INTERPRET,
        name=name,
    )


def step(axis, by):
    size = lax.axis_size(axis)
    return [(i, i + by) for i in range(size) if 0 <= i + by < size]


def exchange(block, per):
    sent = block.reshape(64, per, 1, 128)
    got = lax.all_to_all(sent, PLANE, split_axis=0, concat_axis=0, tiled=True)
    return got.reshape(64 * per, 128)


def shards(spectrum, land_sea, west_index, east_index, current_u, current_v, transfer, wind_rate, dissipation):
    space = lax.axis_index("space")
    place = (space * 2 + lax.axis_index("spec")).astype(jnp.int32)
    spec = spectrum.reshape(COMPS, NCOL)
    sea = land_sea[0]
    wind, damp = wind_rate.reshape(1, NF), dissipation.reshape(1, NF)
    u, v = current_u.reshape(LEV, NCOL), current_v.reshape(LEV, NCOL)
    where = jnp.stack([place, west_index[0, place], east_index[0, place]])
    full, flow = (COMPS, 128), (TILES, 128, 128)

    rows, east, west = kernel(
        rows_source, [full, (TILES, 128), (TILES, 128)], [full], [SM] + [VM] * 5, 340_000_000, 4_000_000, "rows_source"
    )(where, spec, transfer, wind, damp, sea)
    uv, a_rows, b_rows = kernel(
        rows_flow, [(128, 128), flow, flow], [], [VM] * 3, 75_000_000, 2_500_000, "rows_flow"
    )(u, v, FLOW_W)
    from_west = lax.ppermute(east, "grid", step("grid", 1))
    from_east = lax.ppermute(west, "grid", step("grid", -1))
    north = lax.ppermute(rows, PLANE, step(PLANE, 1))
    south = lax.ppermute(rows, PLANE, step(PLANE, -1))
    edges = jnp.concatenate([from_west, from_east], axis=0)
    ghosts = exchange(jnp.broadcast_to(edges[None], (64, 2 * TILES, 128)), 2 * TILES)
    (sent,) = kernel(rows_move, [(64 * MSG, 128)], [], [SM] + [VM] * 8, 10_000_000, 5_000_000, "rows_move")(
        where, rows, north, south, ghosts, a_rows, b_rows, uv, KX
    )
    arrived = exchange(sent, MSG)

    half = (TILES, NROW, 128)
    near, far = kernel(
        columns_source,
        [half, half],
        [(128, 128), flow, full, full],
        [SM] + [VM] * 6,
        340_000_000,
        4_000_000,
        "columns_source",
    )(where, arrived, transfer, wind, damp, sea, KY)
    a_cols, b_cols, drift = kernel(
        columns_flow, [flow, flow, (128, 128)], [], [VM] * 5, 100_000_000, 4_000_000, "columns_flow"
    )(arrived, near, far, FLOW_W, STOKES_T)
    from_west = lax.ppermute(far, EVERY, step(EVERY, 1))
    from_east = lax.ppermute(near, EVERY, step(EVERY, -1))
    at_ends = jnp.stack([place == 0, place == 63])
    steady = jnp.arange(NROW, dtype=jnp.int32)
    picks = [
        (jnp.where(at_ends[n], index[0], steady)[:, None] == steady[None, :]).astype(jnp.float32)
        for n, index in enumerate((west_index, east_index))
    ]
    (sent,) = kernel(
        columns_move,
        [(64 * MSG, 128)],
        [(NROW, 128), (NROW, 128), (128, 128), full],
        [SM] + [VM] * 10,
        10_000_000,
        5_000_000,
        "columns_move",
    )(at_ends.astype(jnp.float32), near, far, from_west, from_east, *picks, a_cols, b_cols, drift, KY)
    arrived = exchange(sent, MSG)

    scalars = lax.dynamic_slice_in_dim(jnp.asarray(SWEEP), place, 1, 0)
    ahead = lax.dynamic_slice_in_dim(jnp.asarray(AHEAD), space, 1, 0)
    waves, stokes = kernel(
        comps_sweep,
        [full, (128, 128)],
        [full, (128, 128)],
        [SM, SM, VM, VM],
        100_000_000,
        2_000_000,
        "comps_sweep",
    )(ahead, scalars, arrived, sea)
    return waves.reshape(1, 1, NF // 2, NROW, NCOL), stokes.reshape(1, 2 * LEV, 1, NCOL)


def solution(mesh):
    rows = P("grid", None, None, PLANE, None)
    depth = P("grid", None, PLANE, None)
    return jax.shard_map(
        shards,
        mesh=mesh,
        in_specs=(rows, P("grid", None, None), P("grid", None), P("grid", None), depth, depth, P(), P(), P()),
        out_specs=(P("grid", "space", "spec", None, None), depth),
        check_vma=False,
    )
```

```python
import jax
import jax.numpy as jnp
import numpy as np
from jax import lax
from jax.experimental import pallas as pl
from jax.experimental.pallas import tpu as pltpu
from jax.sharding import PartitionSpec as P


ND, NF, LEV, NCOL, NROW = 32, 36, 64, 128, 64
COMPS = ND * NF
TILES = COMPS // 128
PLANE = ("space", "spec")
EVERY = ("grid", "space", "spec")
f32 = np.float32
highest = lax.Precision.HIGHEST
MSG = 20
VM = pl.BlockSpec(memory_space=pltpu.VMEM)
SM = pl.BlockSpec(memory_space=pltpu.SMEM)
FETCH = pl.BlockSpec(memory_space=pl.ANY)
TILED = object()
EDGE = 19
INTERPRET = False


def host_tables():
    steps = np.arange(NF).astype(f32)
    radian = f32(0.2199) * f32(1.1) ** steps
    wave = radian * radian / f32(9.81)
    speeds = f32(3.0) * f32(1.1) ** (-steps)
    angles = f32(2.0 * np.pi) * np.arange(ND).astype(f32) / f32(ND)
    depths = -(np.arange(LEV).astype(f32) + f32(0.5))
    decays = np.exp(2.0 * wave[:, None].astype(np.float64) * depths[None, :])
    current = decays / decays.sum(1, keepdims=True)
    drifts = (radian * wave)[:, None] * decays
    drifts = drifts / drifts.sum(0, keepdims=True)
    cosines, sines = np.cos(angles), np.sin(angles)
    return speeds, cosines, sines, current, drifts


SPEEDS, COS, SIN, CURRENT, DRIFTS = host_tables()
CX = (COS[:, None] * SPEEDS[None, :]).astype(f32).reshape(-1)
CY = (SIN[:, None] * SPEEDS[None, :]).astype(f32).reshape(-1)


def scan_table(courant, block, extra):
    rows = []
    for part in (np.maximum(courant, 0), np.maximum(-courant, 0)):
        part = part.astype(np.float64)
        ratio = part / (1.0 + part)
        rows.append(1.0 / (1.0 + part))
        rows.extend(ratio**n for n in range(1, block + 1))
        rows.extend(ratio ** (block * n) for n in extra)
    rows.append(np.maximum(courant, 0))
    rows.append(np.maximum(-courant, 0))
    return np.stack(rows).astype(f32)


KX = scan_table(CX, 16, (2, 4))
KY = scan_table(CY, 8, (2, 4))
KY[-2:] = KX[-2:]
INFLOW = (KX.shape[0] - 2, KY.shape[0] - 2)
HAS = {
    name: [[bool((s * c[128 * k : 128 * k + 128] > 0).any()) for s in (1, -1)] for k in range(TILES)]
    for name, c in (("x", CX), ("y", CY))
}
FLOW_W = np.tile(CURRENT.T, (2, ND)).astype(f32)
FLOW_W = np.ascontiguousarray(FLOW_W.reshape(128, TILES, 128).transpose(1, 0, 2))
GAIN = 2.0 / np.sqrt(float(ND))
STOKES_T = np.concatenate(
    [(DRIFTS.T[:, None, :] * (trig * GAIN)[None, :, None]).reshape(LEV, COMPS) for trig in (COS, SIN)]
).T.astype(f32)


def sweep_scalars():
    c = np.abs(CX.astype(np.float64)).reshape(ND, NF)
    ratio = c / (1 + c)
    cols = [1 / (1 + c), ratio] + [ratio**n for n in (2, 16, 32, 64)]
    cols += [np.zeros_like(c)] * 2
    table = np.stack(cols, -1).reshape(ND * 2, NF // 2, 8)
    return table.reshape(ND * 2, -1).astype(f32)


def fade_rows():
    rows = []
    for courant in (CX, -CX):
        part = np.maximum(courant, 0).astype(np.float64)
        rows.append(np.where(part > 0, np.log(np.maximum(part, 1e-30) / (1 + part)), -1e30))
    rows.append(1 / (1 + np.abs(CX.astype(np.float64))))
    return np.stack(rows).astype(f32)


KY = np.concatenate([KY, fade_rows()])
FADES = KY.shape[0] - 3
SWEEP = sweep_scalars()
AHEAD = (COS >= 0).astype(np.int32)


def down(x, first=None):
    top = jnp.zeros_like(x[:1]) if first is None else first
    return jnp.concatenate([top, x[:-1]], axis=0)


def up(x, last=None):
    end = jnp.zeros_like(x[:1]) if last is None else last
    return jnp.concatenate([x[1:], end], axis=0)


def hop(x, n, forward):
    z = jnp.zeros_like(x[:n])
    return jnp.concatenate([z, x[:-n]] if forward else [x[n:], z], axis=0)


def block_scan(tiles, table, base, lanes, forward):
    block = len(tiles)
    row = lambda n: table[pl.ds(base + n, 1), lanes]
    scale, ratio = row(0), row(1)
    order = list(range(block)) if forward else list(range(block - 1, -1, -1))
    out = [None] * block
    state = None
    for t in order:
        state = scale * tiles[t] if state is None else scale * tiles[t] + ratio * state
        out[t] = state
    ends = state
    ends = ends + row(block) * hop(ends, 1, forward)
    ends = ends + row(block + 1) * hop(ends, 2, forward)
    ends = ends + row(block + 2) * hop(ends, 4, forward)
    carry = hop(ends, 1, forward)
    for n, t in enumerate(order):
        out[t] = out[t] + row(n + 1) * carry
    return out


def sweep(tiles, table, k, has):
    lanes = pl.ds(128 * k, 128)
    size = len(tiles) + 3
    if has[0]:
        tiles = block_scan(tiles, table, 0, lanes, True)
    if has[1]:
        tiles = block_scan(tiles, table, size, lanes, False)
    return tiles


def source_step(spec_ref, transfer, wind, damp, sea_row, out_ref):
    spectra = spec_ref[...]
    redist = jnp.dot(transfer[...], spectra.astype(jnp.bfloat16), preferred_element_type=jnp.float32)
    energy = jnp.sum(spectra * spectra, axis=0, keepdims=True) * (1.0 / COMPS)
    turns = lax.broadcasted_iota(jnp.int32, (2 * NF, NF), 0)
    turns = jnp.where(turns >= NF, turns - NF, turns)
    pick = turns == lax.broadcasted_iota(jnp.int32, (2 * NF, NF), 1)
    wind_col = jnp.sum(jnp.where(pick, wind, 0.0), axis=1, keepdims=True)
    damp_col = jnp.sum(jnp.where(pick, damp, 0.0), axis=1, keepdims=True)
    shrink = sea_row / (1.0 + 0.5 * damp_col * energy)
    first = lax.broadcasted_iota(jnp.int32, (2 * NF, 1), 0) < NF
    for pair in range(ND // 2):
        rows = slice(2 * NF * pair, 2 * NF * (pair + 1))
        near, far = (float(0.25 * (1.0 + COS[2 * pair + n])) for n in range(2))
        gain = 1.0 + jnp.where(first, near, far) * wind_col
        out_ref[rows, :] = (spectra[rows] * gain + 0.5 * redist[rows]) * shrink


def rows_source(place, spec, transfer, wind, damp, land_sea, u, out, spread, work, edges):
    sea_row = land_sea[pl.ds(place[0], 1), :].astype(jnp.float32)
    turned = jnp.concatenate([u[...], u[...]], axis=0).T
    low = lax.broadcasted_iota(jnp.int32, (1, 128), 1) < LEV
    edges[pl.ds(2 * TILES, 1), :] = jnp.where(low, turned[:1], turned[127:])
    source_step(spec, transfer, wind[...], damp[...], sea_row, work)
    for k in range(TILES):
        turned = work[128 * k : 128 * k + 128, :].T
        out[k] = turned
        edges[pl.ds(k, 1), :] = turned[127:]
        edges[pl.ds(TILES + k, 1), :] = turned[:1]
    for n in range(EDGE):
        spread[pl.ds(n, NROW // 2, stride=EDGE), :] = jnp.broadcast_to(edges[pl.ds(n, 1), :], (NROW // 2, 128))


def exact(a, b):
    return jnp.dot(a, b, precision=highest, preferred_element_type=jnp.float32)


def halves(pair):
    low = lax.broadcasted_iota(jnp.int32, pair.shape, 1) < LEV
    return jnp.where(low, pair, 0.0), jnp.where(low, 0.0, pair)


def advect(mid, west, east, north, south, a, b):
    return (
        mid
        - jnp.maximum(a, 0.0) * (mid - west)
        - jnp.maximum(-a, 0.0) * (mid - east)
        - jnp.maximum(b, 0.0) * (mid - north)
        - jnp.maximum(-b, 0.0) * (mid - south)
    )


def rows_move(u, v, table, weights, spec, north, south, out, east_flow, north_flow):
    uv = jnp.concatenate([u.get()[...], v.get()[...]], axis=0).T
    out[pl.ds(TILES, 128, stride=TILES + 1), :] = uv
    both = jnp.concatenate(halves(uv), axis=0)
    table = table.get()
    for k in range(TILES):
        flow = exact(both, weights.get(k)[...])
        east_flow[...] = flow[:128]
        north_flow[...] = flow[128:]
        tile = lambda ref, t: ref[pl.ds(t, 8, stride=16), :]
        now, above, below = (ref.get(k) for ref in (spec, north, south))
        mids = [tile(now, t) for t in range(16)]
        moved = []
        for t in range(16):
            west = mids[t - 1] if t else down(mids[15])
            east = mids[t + 1] if t < 15 else up(mids[0])
            moved.append(
                advect(mids[t], west, east, tile(above, t), tile(below, t), tile(east_flow, t), tile(north_flow, t))
            )
        for t, value in enumerate(sweep(moved, table, k, HAS["x"][k])):
            out[pl.ds(t * (TILES + 1) + k, 8, stride=16 * (TILES + 1)), :] = value


def senders(core, axis):
    n = lax.broadcasted_iota(jnp.int32, (NROW, NROW), axis)
    half = NROW // 2
    return jnp.where(n < half, 2 * n + core, 2 * (n - half) + 1 - core)


def columns_source(
    place, land_sea, wind, damp, table, index_west, index_east, west_own, west_other, east_own, east_other, ends_own,
    ends_other, weights, arrived, transfer, near, far, sea, turned, held, work, inflow,
):
    lane = lax.broadcasted_iota(jnp.int32, (NROW, NCOL), 1)
    core = place[0] % 2
    pick_row = (senders(core, 1) == lax.broadcasted_iota(jnp.int32, (NROW, NROW), 0)).astype(jnp.float32)
    land_sea, table, index_west, index_east = (x.get() for x in (land_sea, table, index_west, index_east))
    picks = [(index[...] == senders(core, 0)).astype(jnp.float32).T for index in (index_west, index_east)]
    edges = [[x.get() for x in pair] for pair in ((west_own, west_other), (east_own, east_other))]
    ends = jnp.concatenate([ends_own.get()[...], ends_other.get()[...]], axis=0)
    arrived = arrived.get() if isinstance(arrived, Fetched) else arrived
    land = land_sea[...].astype(jnp.float32)
    for side in range(2):
        column = jnp.sum(jnp.where(lane == 2 * place[0] + side, land, 0.0), axis=1, keepdims=True)
        sea[NROW * side : NROW * (side + 1), :] = jnp.broadcast_to(column, (NROW, 128))
    behind = (place[0] * 2).astype(jnp.float32)
    ends = jnp.concatenate(halves(exact(pick_row, ends)), axis=0)
    for k in range(TILES):
        lanes = pl.ds(128 * k, 128)
        row = lambda n: table[pl.ds(n, 1), lanes]
        flow = exact(ends, weights.get(k)[...])
        fades = []
        for n, (pick, pair, sign) in enumerate(zip(picks, edges, (1.0, -1.0))):
            speed = jnp.maximum(sign * flow[NROW * n : NROW * (n + 1)], 0.0) + row(INFLOW[1] + n)
            column = jnp.concatenate([ref[pl.ds(k, NROW // 2, stride=TILES), :] for ref in pair], axis=0)
            inflow[NROW * n : NROW * (n + 1), :] = speed * exact(pick, column)
            steps = [behind, behind + 1.0] if n == 0 else [NCOL - 1.0 - behind, NCOL - 2.0 - behind]
            fades.append([row(FADES + 2) * jnp.exp(row(FADES + n) * count) for count in steps])
        for side in range(2):
            tiles = [
                arrived[pl.ds((2 * s + side) * (TILES + 1) + k, 8, stride=16 * (TILES + 1)), :]
                + fades[0][side] * inflow[pl.ds(s, 8, stride=8), :]
                + fades[1][side] * inflow[pl.ds(NROW + s, 8, stride=8), :]
                for s in range(8)
            ]
            for s, value in enumerate(sweep(tiles, table, k, HAS["y"][k])):
                at = pl.ds(NROW * side + s, 8, stride=8)
                turned.at[k][at, :] = value * sea[at, :]
        held[128 * k : 128 * k + 128, :] = turned[k].T
    source_step(held, transfer.get(), wind.get()[...], damp.get()[...], sea[...].T[:1], work)
    for k in range(TILES):
        back = work[128 * k : 128 * k + 128, :].T
        near[k] = back[:NROW]
        far[k] = back[NROW:]


def columns_flow(arrived, near, far, weights, stokes_table, east_flow, north_flow, stokes):
    uv = jnp.concatenate(
        [arrived[pl.ds(TILES + side * (TILES + 1), NROW, stride=MSG), :] for side in range(2)], axis=0
    )
    both = jnp.concatenate(halves(uv), axis=0)
    total = jnp.zeros((128, 128), jnp.float32)
    for k in range(TILES):
        flow = exact(both, weights[k])
        east_flow[k] = flow[:128]
        north_flow[k] = flow[128:]
        spectra = jnp.concatenate([near[k], far[k]], axis=0)
        total = total + exact(spectra, stokes_table[128 * k : 128 * k + 128, :])
    stokes[...] = total


def columns_move(
    place, near, far, from_west, from_east, index_west, index_east, east_flow, north_flow, stokes, table, out,
    west_halo, east_halo, held, turned,
):
    at_end = [place[0] == 0, place[0] == NROW - 1]
    flags = [jnp.where(end, 1.0, 0.0) for end in at_end]
    across, along = (lax.broadcasted_iota(jnp.int32, (NROW, NROW), n) for n in (0, 1))
    picks = [
        (jnp.where(end, jnp.broadcast_to(index[...], (NROW, NROW)), along) == across).astype(jnp.float32).T
        for end, index in zip(at_end, (index_west, index_east))
    ]
    for k in range(TILES):
        west_halo[...] = exact(picks[0], from_west[k])
        east_halo[...] = exact(picks[1], from_east[k])
        lanes = pl.ds(128 * k, 128)
        into = [table[pl.ds(INFLOW[1] + n, 1), lanes] * flags[n] for n in range(2)]
        cells = [[ref.at[k][pl.ds(s, 8, stride=8), :] for s in range(8)] for ref in (near, far)]
        for side in range(2):
            halo = west_halo if side == 0 else east_halo
            moved = []
            for s in range(8):
                at = pl.ds(NROW * side + s, 8, stride=8)
                beyond = halo[pl.ds(s, 8, stride=8), :]
                mids = cells[side]
                north = mids[s - 1] if s else down(mids[7])
                south = mids[s + 1] if s < 7 else up(mids[0])
                west = beyond if side == 0 else cells[0][s]
                east = cells[1][s] if side == 0 else beyond
                value = advect(mids[s], west, east, north, south, east_flow.at[k][at, :], north_flow.at[k][at, :])
                moved.append(value + into[side] * beyond)
            for s, value in enumerate(sweep(moved, table, k, HAS["y"][k])):
                held[pl.ds(NROW * side + s, 8, stride=8), :] = value
        turned[128 * k : 128 * k + 128, :] = held[...].T
    half = NF // 2
    for i in range(half):
        out[pl.ds(i, 64, stride=MSG), :] = turned[pl.ds(i, 64, stride=half), :]
    for side in range(2):
        out[pl.ds(half + side, 64, stride=MSG), :] = stokes[NROW * side : NROW * (side + 1), :]


def comps_sweep(ahead, scalars, arrived, land_sea, waves, stokes, work, rows):
    half = NF // 2
    low = lax.broadcasted_iota(jnp.int32, (8, 128), 1) < NROW

    def solve(forward):
        for i in range(half):
            scale, ratio, ratio2, hop1, hop2, hop4 = (scalars[0, 8 * i + n] for n in range(6))
            tiles = [arrived[pl.ds(t * MSG + i, 8, stride=8 * MSG), :] * scale for t in range(8)]
            order = list(range(8)) if forward else list(range(7, -1, -1))
            state, states = None, {}
            for t in order:
                swapped = pltpu.roll(tiles[t], NROW, 1)
                a = tiles[t] + ratio * swapped
                b = swapped + ratio * tiles[t]
                pair = jnp.where(low, b, a) if forward else jnp.where(low, a, b)
                state = pair if state is None else pair + ratio2 * state
                states[t] = state
            ends = state
            ends = ends + hop1 * hop(ends, 1, forward)
            ends = ends + hop2 * hop(ends, 2, forward)
            ends = ends + hop4 * hop(ends, 4, forward)
            before = hop(ends, 1, forward)
            carry = before
            for t in order:
                carry = ratio2 * carry
                now = states[t] + carry
                other = tiles[t] + ratio * before
                value = jnp.where(low, other, now) if forward else jnp.where(low, now, other)
                work[pl.ds(NROW * i + t, 8, stride=8), :] = value
                before = now

    @pl.when(ahead[0] == 1)
    def _():
        solve(True)

    @pl.when(ahead[0] == 0)
    def _():
        solve(False)

    land = land_sea[...].astype(jnp.float32)
    which = lax.broadcasted_iota(jnp.int32, (128, 256), 0)
    there = lax.broadcasted_iota(jnp.int32, (128, 256), 1)
    spread = [
        (2 * jnp.where(which >= NROW, which - NROW, which) + side + jnp.where(which >= NROW, 128, 0) == there)
        .astype(jnp.float32)
        .astype(jnp.bfloat16)
        for side in range(2)
    ]
    for pair in range(half // 2):
        both = work[128 * pair : 128 * pair + 128, :].T
        total = jnp.zeros((NROW, 256), jnp.float32)
        for side in range(2):
            left = both[NROW * side : NROW * (side + 1)]
            for n in range(3):
                part = left.astype(jnp.bfloat16)
                total = total + jnp.dot(part, spread[side], preferred_element_type=jnp.float32)
                if n < 2:
                    left = left - part.astype(jnp.float32)
        for n in range(2):
            i = 2 * pair + n
            waves[NROW * i : NROW * (i + 1), :] = total[:, 128 * n : 128 * n + 128] * land
    for side in range(2):
        rows[pl.ds(side, 64, stride=2), :] = arrived[pl.ds(half + side, 64, stride=MSG), :]
    stokes[...] = rows[...].T


class Fetched:
    def __init__(self, source, buffer, sem, tiled):
        self.ref, self.tiled = buffer, tiled
        if tiled:
            parts = range(source.shape[0])
            self.copies = [pltpu.make_async_copy(source.at[k], buffer.at[k], sem.at[k]) for k in parts]
        else:
            self.copies = [pltpu.make_async_copy(source, buffer, sem.at[0])]

    def get(self, k=0):
        self.copies[k].wait()
        return self.ref.at[k] if self.tiled else self.ref


def kernel(body, outs, scratch, specs, args, flops, nbytes, limit=60):
    late = [n for n, spec in enumerate(specs) if spec is FETCH or spec is TILED]

    def whole(*refs):
        size = len(refs) - 2 * len(late)
        refs, buffers, sems = list(refs[:size]), refs[size : size + len(late)], refs[size + len(late) :]
        for at, buffer, sem in zip(late, buffers, sems):
            refs[at] = Fetched(refs[at], buffer, sem, specs[at] is TILED)
        for k in range(TILES):
            for at in late:
                if k < len(refs[at].copies):
                    refs[at].copies[k].start()
        body(*refs)

    buffers = [pltpu.VMEM(args[at].shape, args[at].dtype) for at in late]
    sems = [pltpu.SemaphoreType.DMA((TILES if specs[at] is TILED else 1,)) for at in late]
    return pl.pallas_call(
        whole if late else body,
        out_shape=[jax.ShapeDtypeStruct(s, jnp.float32) for s in outs],
        in_specs=[pl.BlockSpec(memory_space=pl.ANY) if spec is TILED else spec for spec in specs],
        out_specs=[VM] * len(outs),
        scratch_shapes=[pltpu.VMEM(s, jnp.float32) for s in scratch] + buffers + sems,
        compiler_params=pltpu.CompilerParams(vmem_limit_bytes=limit << 20),
        cost_estimate=pl.CostEstimate(flops=flops, bytes_accessed=nbytes, transcendentals=0),
        interpret=INTERPRET,
    )(*args)


def step(axis, by):
    size = lax.axis_size(axis)
    return [(i, i + by) for i in range(size) if 0 <= i + by < size]


def exchange(block, per, axes=PLANE):
    sent = block.reshape(lax.axis_size(axes), per, 1, 128)
    got = lax.all_to_all(sent, axes, split_axis=0, concat_axis=0, tiled=True)
    return got.reshape(-1, 128)


def model(spectrum, land_sea, west_index, east_index, current_u, current_v, transfer, wind_rate, dissipation):
    space = lax.axis_index("space").astype(jnp.int32)
    place = space * 2 + lax.axis_index("spec").astype(jnp.int32)
    at = place.reshape(1)
    spec = spectrum.reshape(COMPS, NCOL)
    sea = land_sea[0]
    wind, damp = wind_rate.reshape(1, NF), dissipation.reshape(1, NF)
    u, v = current_u.reshape(LEV, NCOL), current_v.reshape(LEV, NCOL)
    full, flow, half, square = (COMPS, 128), (TILES, 128, 128), (TILES, NROW, 128), (128, 128)
    weights = jnp.asarray(FLOW_W)

    rows, spread = kernel(
        rows_source,
        [flow, (NROW // 2 * EDGE, 128)],
        [full, (24, 128)],
        [SM, VM, VM, VM, VM, VM, VM],
        [at, spec, transfer, wind, damp, sea, u],
        340_000_000,
        4_000_000,
    )
    north = lax.ppermute(rows, PLANE, step(PLANE, 1))
    south = lax.ppermute(rows, PLANE, step(PLANE, -1))
    own = exchange(spread, EDGE, "space").reshape(NROW // 2, EDGE, 1, 128)
    (sent,) = kernel(
        rows_move,
        [(64 * MSG, 128)],
        [square, square],
        [FETCH, FETCH, FETCH, TILED, TILED, TILED, TILED],
        [u, v, jnp.asarray(KX), weights, rows, north, south],
        90_000_000,
        5_000_000,
    )
    arrived = exchange(sent, MSG)

    def shifted(part, by):
        size = lax.axis_size("grid")
        chips = step("grid", by) if by else [(i, i) for i in range(size)]
        cross = [(2 * i + 1 - core, 2 * j + core) for i, j in chips for core in range(2)]
        same = lax.ppermute(part, "grid", chips) if by else part
        other = lax.ppermute(part, ("grid", "spec"), cross)
        return [x.reshape(-1, 128) for x in (same, other)]

    edges = shifted(own[:, :TILES], 1) + shifted(own[:, TILES : 2 * TILES], -1) + shifted(own[:, 2 * TILES :], 0)

    near, far = kernel(
        columns_source,
        [half, half],
        [square, flow, full, full, square],
        [SM] + [FETCH] * 12 + [TILED, FETCH, FETCH],
        [at, sea, wind, damp, jnp.asarray(KY), west_index, east_index, *edges, weights, arrived, transfer],
        400_000_000,
        7_000_000,
        60,
    )
    a_cols, b_cols, drift = kernel(
        columns_flow,
        [flow, flow, square],
        [],
        [VM] * 5,
        [arrived, near, far, weights, jnp.asarray(STOKES_T)],
        100_000_000,
        4_000_000,
        32,
    )
    from_west = lax.ppermute(far, EVERY, step(EVERY, 1))
    from_east = lax.ppermute(near, EVERY, step(EVERY, -1))
    (sent,) = kernel(
        columns_move,
        [(64 * MSG, 128)],
        [(NROW, 128), (NROW, 128), square, full],
        [SM] + [VM] * 10,
        [at, near, far, from_west, from_east, west_index, east_index, a_cols, b_cols, drift, jnp.asarray(KY)],
        10_000_000,
        5_000_000,
        32,
    )
    arrived = exchange(sent, MSG)

    scalars = lax.dynamic_slice_in_dim(jnp.asarray(SWEEP), place, 1, 0)
    ahead = lax.dynamic_slice_in_dim(jnp.asarray(AHEAD), space, 1, 0)
    waves, stokes = kernel(
        comps_sweep,
        [full, square],
        [full, square],
        [SM, SM, VM, VM],
        [ahead, scalars, arrived, sea],
        100_000_000,
        2_000_000,
        32,
    )
    return waves.reshape(1, 1, NF // 2, NROW, NCOL), stokes.reshape(1, 2 * LEV, 1, NCOL)


def solution(mesh):
    rows = P("grid", None, None, PLANE, None)
    depth = P("grid", None, PLANE, None)
    return jax.shard_map(
        model,
        mesh=mesh,
        in_specs=(rows, P("grid", None, None), P("grid", None), P("grid", None), depth, depth, P(), P(), P()),
        out_specs=(P("grid", "space", "spec", None, None), depth),
        check_vma=False,
    )
```

```python
import jax
import jax.numpy as jnp
import numpy as np
from jax import lax
from jax.experimental import pallas as pl
from jax.experimental.pallas import tpu as pltpu
from jax.sharding import PartitionSpec as P


ND, NF, LEV, NCOL, NROW = 32, 36, 64, 128, 64
COMPS = ND * NF
TILES = COMPS // 128
PLANE = ("space", "spec")
EVERY = ("grid", "space", "spec")
f32 = np.float32
highest = lax.Precision.HIGHEST
INFLOW_LIMIT = 60
MSG = 20
VM = pl.BlockSpec(memory_space=pltpu.VMEM)
SM = pl.BlockSpec(memory_space=pltpu.SMEM)
FETCH = pl.BlockSpec(memory_space=pl.ANY)
TILED = object()
EDGE = 19
INTERPRET = False


def host_tables():
    steps = np.arange(NF).astype(f32)
    radian = f32(0.2199) * f32(1.1) ** steps
    wave = radian * radian / f32(9.81)
    speeds = f32(3.0) * f32(1.1) ** (-steps)
    angles = f32(2.0 * np.pi) * np.arange(ND).astype(f32) / f32(ND)
    depths = -(np.arange(LEV).astype(f32) + f32(0.5))
    decays = np.exp(2.0 * wave[:, None].astype(np.float64) * depths[None, :])
    current = decays / decays.sum(1, keepdims=True)
    drifts = (radian * wave)[:, None] * decays
    drifts = drifts / drifts.sum(0, keepdims=True)
    cosines, sines = np.cos(angles), np.sin(angles)
    return speeds, cosines, sines, current, drifts


SPEEDS, COS, SIN, CURRENT, DRIFTS = host_tables()
CX = (COS[:, None] * SPEEDS[None, :]).astype(f32).reshape(-1)
CY = (SIN[:, None] * SPEEDS[None, :]).astype(f32).reshape(-1)


def scan_table(courant, block, extra):
    rows = []
    for part in (np.maximum(courant, 0), np.maximum(-courant, 0)):
        part = part.astype(np.float64)
        ratio = part / (1.0 + part)
        rows.append(1.0 / (1.0 + part))
        rows.extend(ratio**n for n in range(1, block + 1))
        rows.extend(ratio ** (block * n) for n in extra)
    rows.append(np.maximum(courant, 0))
    rows.append(np.maximum(-courant, 0))
    return np.stack(rows).astype(f32)


KX = scan_table(CX, 16, (2, 4))
KY = scan_table(CY, 8, (2, 4))
KY[-2:] = KX[-2:]
INFLOW = (KX.shape[0] - 2, KY.shape[0] - 2)
HAS = {
    name: [[bool((s * c[128 * k : 128 * k + 128] > 0).any()) for s in (1, -1)] for k in range(TILES)]
    for name, c in (("x", CX), ("y", CY))
}
FLOW_W = np.tile(CURRENT.T, (2, ND)).astype(f32)
GAIN = 2.0 / np.sqrt(float(ND))
STOKES_T = np.concatenate(
    [(DRIFTS.T[:, None, :] * (trig * GAIN)[None, :, None]).reshape(LEV, COMPS) for trig in (COS, SIN)]
).T.astype(f32)


def sweep_scalars():
    c = np.abs(CX.astype(np.float64)).reshape(ND, NF)
    ratio = c / (1 + c)
    cols = [1 / (1 + c), ratio] + [ratio**n for n in (2, 16, 32, 64)]
    cols += [np.zeros_like(c)] * 2
    table = np.stack(cols, -1).reshape(ND * 2, NF // 2, 8)
    return table.reshape(ND * 2, -1).astype(f32)


def fade_rows():
    rows = []
    for courant in (CX, -CX):
        part = np.maximum(courant, 0).astype(np.float64)
        rows.append(np.where(part > 0, np.log(np.maximum(part, 1e-30) / (1 + part)), -1e30))
    rows.append(1 / (1 + np.abs(CX.astype(np.float64))))
    return np.stack(rows).astype(f32)


KY = np.concatenate([KY, fade_rows()])
FADES = KY.shape[0] - 3
SWEEP = sweep_scalars()
AHEAD = (COS >= 0).astype(np.int32)


def down(x, first=None):
    top = jnp.zeros_like(x[:1]) if first is None else first
    return jnp.concatenate([top, x[:-1]], axis=0)


def up(x, last=None):
    end = jnp.zeros_like(x[:1]) if last is None else last
    return jnp.concatenate([x[1:], end], axis=0)


def hop(x, n, forward):
    z = jnp.zeros_like(x[:n])
    return jnp.concatenate([z, x[:-n]] if forward else [x[n:], z], axis=0)


def block_scan(tiles, table, base, lanes, forward):
    block = len(tiles)
    row = lambda n: table[pl.ds(base + n, 1), lanes]
    scale, ratio = row(0), row(1)
    order = list(range(block)) if forward else list(range(block - 1, -1, -1))
    out = [None] * block
    state = None
    for t in order:
        state = scale * tiles[t] if state is None else scale * tiles[t] + ratio * state
        out[t] = state
    ends = state
    ends = ends + row(block) * hop(ends, 1, forward)
    ends = ends + row(block + 1) * hop(ends, 2, forward)
    ends = ends + row(block + 2) * hop(ends, 4, forward)
    carry = hop(ends, 1, forward)
    for n, t in enumerate(order):
        out[t] = out[t] + row(n + 1) * carry
    return out


def sweep(tiles, table, k, has):
    lanes = pl.ds(128 * k, 128)
    size = len(tiles) + 3
    if has[0]:
        tiles = block_scan(tiles, table, 0, lanes, True)
    if has[1]:
        tiles = block_scan(tiles, table, size, lanes, False)
    return tiles


def source_step(spec_ref, transfer, wind, damp, sea_row, out_ref):
    spectra = spec_ref[...]
    redist = jnp.dot(transfer[...], spectra.astype(jnp.bfloat16), preferred_element_type=jnp.float32)
    energy = jnp.sum(spectra * spectra, axis=0, keepdims=True) * (1.0 / COMPS)
    turns = lax.broadcasted_iota(jnp.int32, (2 * NF, NF), 0)
    turns = jnp.where(turns >= NF, turns - NF, turns)
    pick = turns == lax.broadcasted_iota(jnp.int32, (2 * NF, NF), 1)
    wind_col = jnp.sum(jnp.where(pick, wind, 0.0), axis=1, keepdims=True)
    damp_col = jnp.sum(jnp.where(pick, damp, 0.0), axis=1, keepdims=True)
    shrink = sea_row / (1.0 + 0.5 * damp_col * energy)
    first = lax.broadcasted_iota(jnp.int32, (2 * NF, 1), 0) < NF
    for pair in range(ND // 2):
        rows = slice(2 * NF * pair, 2 * NF * (pair + 1))
        near, far = (float(0.25 * (1.0 + COS[2 * pair + n])) for n in range(2))
        gain = 1.0 + jnp.where(first, near, far) * wind_col
        out_ref[rows, :] = (spectra[rows] * gain + 0.5 * redist[rows]) * shrink


def rows_source(place, spec, transfer, wind, damp, land_sea, u, out, spread, work, edges):
    sea_row = land_sea[pl.ds(place[0], 1), :].astype(jnp.float32)
    turned = jnp.concatenate([u[...], u[...]], axis=0).T
    low = lax.broadcasted_iota(jnp.int32, (1, 128), 1) < LEV
    edges[pl.ds(2 * TILES, 1), :] = jnp.where(low, turned[:1], turned[127:])
    source_step(spec, transfer, wind[...], damp[...], sea_row, work)
    for k in range(TILES):
        turned = work[128 * k : 128 * k + 128, :].T
        out[k] = turned
        edges[pl.ds(k, 1), :] = turned[127:]
        edges[pl.ds(TILES + k, 1), :] = turned[:1]
    for n in range(EDGE):
        spread[pl.ds(n, NROW // 2, stride=EDGE), :] = jnp.broadcast_to(edges[pl.ds(n, 1), :], (NROW // 2, 128))


def exact(a, b):
    return jnp.dot(a, b, precision=highest, preferred_element_type=jnp.float32)


def halves(pair):
    low = lax.broadcasted_iota(jnp.int32, pair.shape, 1) < LEV
    return jnp.where(low, pair, 0.0), jnp.where(low, 0.0, pair)


def advect(mid, west, east, north, south, a, b):
    return (
        mid
        - jnp.maximum(a, 0.0) * (mid - west)
        - jnp.maximum(-a, 0.0) * (mid - east)
        - jnp.maximum(b, 0.0) * (mid - north)
        - jnp.maximum(-b, 0.0) * (mid - south)
    )


def rows_move(u, v, weights, table, spec, north, south, out, flow):
    uv = jnp.concatenate([u.get()[...], v.get()[...]], axis=0).T
    out[pl.ds(TILES, 128, stride=TILES + 1), :] = uv
    both = exact(jnp.concatenate(halves(uv), axis=0), weights.get()[...])
    for k in range(TILES):
        flow[k] = both[:, 128 * k : 128 * k + 128]
    table = table.get()
    for k in range(TILES):
        tile = lambda ref, t: ref[pl.ds(t, 8, stride=16), :]
        now, above, below = (ref.get(k) for ref in (spec, north, south))
        mids = [tile(now, t) for t in range(16)]
        moved = []
        for t in range(16):
            west = mids[t - 1] if t else down(mids[15])
            east = mids[t + 1] if t < 15 else up(mids[0])
            along, across = tile(flow.at[k], t), tile(flow.at[k], 128 + t)
            moved.append(advect(mids[t], west, east, tile(above, t), tile(below, t), along, across))
        for t, value in enumerate(sweep(moved, table, k, HAS["x"][k])):
            out[pl.ds(t * (TILES + 1) + k, 8, stride=16 * (TILES + 1)), :] = value


def senders(core, axis):
    n = lax.broadcasted_iota(jnp.int32, (NROW, NROW), axis)
    half = NROW // 2
    return jnp.where(n < half, 2 * n + core, 2 * (n - half) + 1 - core)


def columns_inflow(
    place, wide, table, index_west, index_east, west_own, west_other, east_own, east_other, ends_own, ends_other, out,
    flow,
):
    core = place[0] % 2
    pick_row = (senders(core, 1) == lax.broadcasted_iota(jnp.int32, (NROW, NROW), 0)).astype(jnp.float32)
    ends = exact(pick_row, jnp.concatenate([ends_own[...], ends_other[...]], axis=0))
    flow[...] = exact(jnp.concatenate(halves(ends), axis=0), wide[...])
    behind = (place[0] * 2).astype(jnp.float32)
    added = [[], []]
    for n, (index, own, other, sign) in enumerate(
        ((index_west, west_own, west_other, 1.0), (index_east, east_own, east_other, -1.0))
    ):
        pick = (index[...] == senders(core, 0)).astype(jnp.float32).T
        columns = jnp.concatenate(
            [
                jnp.concatenate([ref[pl.ds(k, NROW // 2, stride=TILES), :] for ref in (own, other)], axis=0)
                for k in range(TILES)
            ],
            axis=1,
        )
        speed = jnp.maximum(sign * flow[NROW * n : NROW * (n + 1), :], 0.0) + table[pl.ds(INFLOW[1] + n, 1), :]
        inflow = speed * exact(pick, columns)
        steps = [behind, behind + 1.0] if n == 0 else [NCOL - 1.0 - behind, NCOL - 2.0 - behind]
        for side in range(2):
            fade = table[pl.ds(FADES + 2, 1), :] * jnp.exp(table[pl.ds(FADES + n, 1), :] * steps[side])
            added[side].append(fade * inflow)
    for side in range(2):
        total = added[side][0] + added[side][1]
        for k in range(TILES):
            out[k, NROW * side : NROW * (side + 1), :] = total[:, 128 * k : 128 * k + 128]


def columns_source(
    place, land_sea, wind, damp, table, inflow, arrived, transfer, near, far, sea, turned, held, work
):
    lane = lax.broadcasted_iota(jnp.int32, (NROW, NCOL), 1)
    land = land_sea[...].astype(jnp.float32)
    for side in range(2):
        column = jnp.sum(jnp.where(lane == 2 * place[0] + side, land, 0.0), axis=1, keepdims=True)
        sea[NROW * side : NROW * (side + 1), :] = jnp.broadcast_to(column, (NROW, 128))
    for k in range(TILES):
        for side in range(2):
            places = [pl.ds(NROW * side + s, 8, stride=8) for s in range(8)]
            tiles = [
                arrived[pl.ds((2 * s + side) * (TILES + 1) + k, 8, stride=16 * (TILES + 1)), :]
                + inflow.at[k][places[s], :]
                for s in range(8)
            ]
            for s, value in enumerate(sweep(tiles, table, k, HAS["y"][k])):
                turned.at[k][places[s], :] = value * sea[places[s], :]
        held[128 * k : 128 * k + 128, :] = turned[k].T
    source_step(held, transfer, wind[...], damp[...], sea[...].T[:1], work)
    for k in range(TILES):
        back = work[128 * k : 128 * k + 128, :].T
        near[k] = back[:NROW]
        far[k] = back[NROW:]


def columns_flow(arrived, near, far, weights, stokes_table, east_flow, north_flow, stokes):
    uv = jnp.concatenate(
        [arrived[pl.ds(TILES + side * (TILES + 1), NROW, stride=MSG), :] for side in range(2)], axis=0
    )
    both = exact(jnp.concatenate(halves(uv), axis=0), weights[...])
    total = jnp.zeros((128, 128), jnp.float32)
    for k in range(TILES):
        east_flow[k] = both[:128, 128 * k : 128 * k + 128]
        north_flow[k] = both[128:, 128 * k : 128 * k + 128]
        spectra = jnp.concatenate([near[k], far[k]], axis=0)
        total = total + exact(spectra, stokes_table[128 * k : 128 * k + 128, :])
    stokes[...] = total


def columns_move(
    place, near, far, from_west, from_east, index_west, index_east, east_flow, north_flow, stokes, table, out,
    west_halo, east_halo, held, turned,
):
    at_end = [place[0] == 0, place[0] == NROW - 1]
    flags = [jnp.where(end, 1.0, 0.0) for end in at_end]
    across, along = (lax.broadcasted_iota(jnp.int32, (NROW, NROW), n) for n in (0, 1))
    picks = [
        (jnp.where(end, jnp.broadcast_to(index[...], (NROW, NROW)), along) == across).astype(jnp.float32).T
        for end, index in zip(at_end, (index_west, index_east))
    ]
    for k in range(TILES):
        west_halo[...] = exact(picks[0], from_west[k])
        east_halo[...] = exact(picks[1], from_east[k])
        lanes = pl.ds(128 * k, 128)
        into = [table[pl.ds(INFLOW[1] + n, 1), lanes] * flags[n] for n in range(2)]
        cells = [[ref.at[k][pl.ds(s, 8, stride=8), :] for s in range(8)] for ref in (near, far)]
        for side in range(2):
            halo = west_halo if side == 0 else east_halo
            moved = []
            for s in range(8):
                at = pl.ds(NROW * side + s, 8, stride=8)
                beyond = halo[pl.ds(s, 8, stride=8), :]
                mids = cells[side]
                north = mids[s - 1] if s else down(mids[7])
                south = mids[s + 1] if s < 7 else up(mids[0])
                west = beyond if side == 0 else cells[0][s]
                east = cells[1][s] if side == 0 else beyond
                value = advect(mids[s], west, east, north, south, east_flow.at[k][at, :], north_flow.at[k][at, :])
                moved.append(value + into[side] * beyond)
            for s, value in enumerate(sweep(moved, table, k, HAS["y"][k])):
                held[pl.ds(NROW * side + s, 8, stride=8), :] = value
        turned[128 * k : 128 * k + 128, :] = held[...].T
    half = NF // 2
    for i in range(half):
        out[pl.ds(i, 64, stride=MSG), :] = turned[pl.ds(i, 64, stride=half), :]
    for side in range(2):
        out[pl.ds(half + side, 64, stride=MSG), :] = stokes[NROW * side : NROW * (side + 1), :]


def comps_sweep(ahead, scalars, arrived, land_sea, waves, stokes, work, rows):
    half = NF // 2
    low = lax.broadcasted_iota(jnp.int32, (8, 128), 1) < NROW

    def solve(forward):
        for i in range(half):
            scale, ratio, ratio2, hop1, hop2, hop4 = (scalars[0, 8 * i + n] for n in range(6))
            tiles = [arrived[pl.ds(t * MSG + i, 8, stride=8 * MSG), :] * scale for t in range(8)]
            order = list(range(8)) if forward else list(range(7, -1, -1))
            state, states = None, {}
            for t in order:
                swapped = pltpu.roll(tiles[t], NROW, 1)
                a = tiles[t] + ratio * swapped
                b = swapped + ratio * tiles[t]
                pair = jnp.where(low, b, a) if forward else jnp.where(low, a, b)
                state = pair if state is None else pair + ratio2 * state
                states[t] = state
            ends = state
            ends = ends + hop1 * hop(ends, 1, forward)
            ends = ends + hop2 * hop(ends, 2, forward)
            ends = ends + hop4 * hop(ends, 4, forward)
            before = hop(ends, 1, forward)
            carry = before
            for t in order:
                carry = ratio2 * carry
                now = states[t] + carry
                other = tiles[t] + ratio * before
                value = jnp.where(low, other, now) if forward else jnp.where(low, now, other)
                work[pl.ds(NROW * i + t, 8, stride=8), :] = value
                before = now

    @pl.when(ahead[0] == 1)
    def _():
        solve(True)

    @pl.when(ahead[0] == 0)
    def _():
        solve(False)

    land = land_sea[...].astype(jnp.float32)
    which = lax.broadcasted_iota(jnp.int32, (128, 256), 0)
    there = lax.broadcasted_iota(jnp.int32, (128, 256), 1)
    spread = [
        (2 * jnp.where(which >= NROW, which - NROW, which) + side + jnp.where(which >= NROW, 128, 0) == there)
        .astype(jnp.float32)
        .astype(jnp.bfloat16)
        for side in range(2)
    ]
    for pair in range(half // 2):
        both = work[128 * pair : 128 * pair + 128, :].T
        total = jnp.zeros((NROW, 256), jnp.float32)
        for side in range(2):
            left = both[NROW * side : NROW * (side + 1)]
            for n in range(3):
                part = left.astype(jnp.bfloat16)
                total = total + jnp.dot(part, spread[side], preferred_element_type=jnp.float32)
                if n < 2:
                    left = left - part.astype(jnp.float32)
        for n in range(2):
            i = 2 * pair + n
            waves[NROW * i : NROW * (i + 1), :] = total[:, 128 * n : 128 * n + 128] * land
    for side in range(2):
        rows[pl.ds(side, 64, stride=2), :] = arrived[pl.ds(half + side, 64, stride=MSG), :]
    stokes[...] = rows[...].T


class Fetched:
    def __init__(self, source, buffer, sem, tiled):
        self.ref, self.tiled = buffer, tiled
        if tiled:
            parts = range(source.shape[0])
            self.copies = [pltpu.make_async_copy(source.at[k], buffer.at[k], sem.at[k]) for k in parts]
        else:
            self.copies = [pltpu.make_async_copy(source, buffer, sem.at[0])]

    def get(self, k=0):
        self.copies[k].wait()
        return self.ref.at[k] if self.tiled else self.ref


def kernel(body, outs, scratch, specs, args, flops, nbytes, limit=60):
    late = [n for n, spec in enumerate(specs) if spec is FETCH or spec is TILED]

    def whole(*refs):
        size = len(refs) - 2 * len(late)
        refs, buffers, sems = list(refs[:size]), refs[size : size + len(late)], refs[size + len(late) :]
        for at, buffer, sem in zip(late, buffers, sems):
            refs[at] = Fetched(refs[at], buffer, sem, specs[at] is TILED)
        for k in range(TILES):
            for at in late:
                if k < len(refs[at].copies):
                    refs[at].copies[k].start()
        body(*refs)

    buffers = [pltpu.VMEM(args[at].shape, args[at].dtype) for at in late]
    sems = [pltpu.SemaphoreType.DMA((TILES if specs[at] is TILED else 1,)) for at in late]
    return pl.pallas_call(
        whole if late else body,
        out_shape=[jax.ShapeDtypeStruct(s, jnp.float32) for s in outs],
        in_specs=[pl.BlockSpec(memory_space=pl.ANY) if spec is TILED else spec for spec in specs],
        out_specs=[VM] * len(outs),
        scratch_shapes=[pltpu.VMEM(s, jnp.float32) for s in scratch] + buffers + sems,
        compiler_params=pltpu.CompilerParams(vmem_limit_bytes=limit << 20),
        cost_estimate=pl.CostEstimate(flops=flops, bytes_accessed=nbytes, transcendentals=0),
        interpret=INTERPRET,
    )(*args)


def step(axis, by):
    size = lax.axis_size(axis)
    return [(i, i + by) for i in range(size) if 0 <= i + by < size]


def exchange(block, per, axes=PLANE):
    sent = block.reshape(lax.axis_size(axes), per, 1, 128)
    got = lax.all_to_all(sent, axes, split_axis=0, concat_axis=0, tiled=True)
    return got.reshape(-1, 128)


def model(spectrum, land_sea, west_index, east_index, current_u, current_v, transfer, wind_rate, dissipation):
    space = lax.axis_index("space").astype(jnp.int32)
    place = space * 2 + lax.axis_index("spec").astype(jnp.int32)
    at = place.reshape(1)
    spec = spectrum.reshape(COMPS, NCOL)
    sea = land_sea[0]
    wind, damp = wind_rate.reshape(1, NF), dissipation.reshape(1, NF)
    u, v = current_u.reshape(LEV, NCOL), current_v.reshape(LEV, NCOL)
    full, flow, half, square = (COMPS, 128), (TILES, 128, 128), (TILES, NROW, 128), (128, 128)
    weights = jnp.asarray(FLOW_W)

    rows, spread = kernel(
        rows_source,
        [flow, (NROW // 2 * EDGE, 128)],
        [full, (24, 128)],
        [SM, VM, VM, VM, VM, VM, VM],
        [at, spec, transfer, wind, damp, sea, u],
        340_000_000,
        4_000_000,
    )
    north = lax.ppermute(rows, PLANE, step(PLANE, 1))
    south = lax.ppermute(rows, PLANE, step(PLANE, -1))
    own = exchange(spread, EDGE, "space").reshape(NROW // 2, EDGE, 1, 128)
    (sent,) = kernel(
        rows_move,
        [(64 * MSG, 128)],
        [(TILES, 256, 128)],
        [FETCH, FETCH, FETCH, FETCH, TILED, TILED, TILED],
        [u, v, weights, jnp.asarray(KX), rows, north, south],
        90_000_000,
        5_000_000,
    )
    arrived = exchange(sent, MSG)

    def shifted(part, by):
        size = lax.axis_size("grid")
        chips = step("grid", by) if by else [(i, i) for i in range(size)]
        cross = [(2 * i + 1 - core, 2 * j + core) for i, j in chips for core in range(2)]
        same = lax.ppermute(part, "grid", chips) if by else part
        other = lax.ppermute(part, ("grid", "spec"), cross)
        return [x.reshape(-1, 128) for x in (same, other)]

    edges = shifted(own[:, :TILES], 1) + shifted(own[:, TILES : 2 * TILES], -1) + shifted(own[:, 2 * TILES :], 0)

    table = jnp.asarray(KY)
    (inflow,) = kernel(
        columns_inflow,
        [flow],
        [(128, COMPS)],
        [SM] + [VM] * 10,
        [at, weights, table, west_index, east_index, *edges],
        60_000_000,
        3_000_000,
        INFLOW_LIMIT,
    )
    near, far = kernel(
        columns_source,
        [half, half],
        [square, flow, full, full],
        [SM] + [VM] * 7,
        [at, sea, wind, damp, table, inflow, arrived, transfer],
        400_000_000,
        7_000_000,
        32,
    )
    a_cols, b_cols, drift = kernel(
        columns_flow,
        [flow, flow, square],
        [],
        [VM] * 5,
        [arrived, near, far, weights, jnp.asarray(STOKES_T)],
        100_000_000,
        4_000_000,
        32,
    )
    from_west = lax.ppermute(far, EVERY, step(EVERY, 1))
    from_east = lax.ppermute(near, EVERY, step(EVERY, -1))
    (sent,) = kernel(
        columns_move,
        [(64 * MSG, 128)],
        [(NROW, 128), (NROW, 128), square, full],
        [SM] + [VM] * 10,
        [at, near, far, from_west, from_east, west_index, east_index, a_cols, b_cols, drift, table],
        10_000_000,
        5_000_000,
        32,
    )
    arrived = exchange(sent, MSG)

    scalars = lax.dynamic_slice_in_dim(jnp.asarray(SWEEP), place, 1, 0)
    ahead = lax.dynamic_slice_in_dim(jnp.asarray(AHEAD), space, 1, 0)
    waves, stokes = kernel(
        comps_sweep,
        [full, square],
        [full, square],
        [SM, SM, VM, VM],
        [ahead, scalars, arrived, sea],
        100_000_000,
        2_000_000,
        32,
    )
    return waves.reshape(1, 1, NF // 2, NROW, NCOL), stokes.reshape(1, 2 * LEV, 1, NCOL)


def solution(mesh):
    rows = P("grid", None, None, PLANE, None)
    depth = P("grid", None, PLANE, None)
    return jax.shard_map(
        model,
        mesh=mesh,
        in_specs=(rows, P("grid", None, None), P("grid", None), P("grid", None), depth, depth, P(), P(), P()),
        out_specs=(P("grid", "space", "spec", None, None), depth),
        check_vma=False,
    )
```

```python
import jax
import jax.numpy as jnp
import numpy as np
from jax import lax
from jax.experimental import pallas as pl
from jax.experimental.pallas import tpu as pltpu
from jax.sharding import PartitionSpec as P


ND, NF, LEV, NCOL, NROW = 32, 36, 64, 128, 64
COMPS = ND * NF
TILES = COMPS // 128
PLANE = ("space", "spec")
EVERY = ("grid", "space", "spec")
f32 = np.float32
highest = lax.Precision.HIGHEST
INFLOW_LIMIT = 60
MSG = 20
VM = pl.BlockSpec(memory_space=pltpu.VMEM)
SM = pl.BlockSpec(memory_space=pltpu.SMEM)
FETCH = pl.BlockSpec(memory_space=pl.ANY)
TILED = object()
EDGE = 19
INTERPRET = False


def host_tables():
    steps = np.arange(NF).astype(f32)
    radian = f32(0.2199) * f32(1.1) ** steps
    wave = radian * radian / f32(9.81)
    speeds = f32(3.0) * f32(1.1) ** (-steps)
    angles = f32(2.0 * np.pi) * np.arange(ND).astype(f32) / f32(ND)
    depths = -(np.arange(LEV).astype(f32) + f32(0.5))
    decays = np.exp(2.0 * wave[:, None].astype(np.float64) * depths[None, :])
    current = decays / decays.sum(1, keepdims=True)
    drifts = (radian * wave)[:, None] * decays
    drifts = drifts / drifts.sum(0, keepdims=True)
    cosines, sines = np.cos(angles), np.sin(angles)
    return speeds, cosines, sines, current, drifts


SPEEDS, COS, SIN, CURRENT, DRIFTS = host_tables()
CX = (COS[:, None] * SPEEDS[None, :]).astype(f32).reshape(-1)
CY = (SIN[:, None] * SPEEDS[None, :]).astype(f32).reshape(-1)


def scan_table(courant, block, extra):
    rows = []
    for part in (np.maximum(courant, 0), np.maximum(-courant, 0)):
        part = part.astype(np.float64)
        ratio = part / (1.0 + part)
        rows.append(1.0 / (1.0 + part))
        rows.extend(ratio**n for n in range(1, block + 1))
        rows.extend(ratio ** (block * n) for n in extra)
    rows.append(np.maximum(courant, 0))
    rows.append(np.maximum(-courant, 0))
    return np.stack(rows).astype(f32)


KX = scan_table(CX, 16, (2, 4))
KY = scan_table(CY, 8, (2, 4))
KY[-2:] = KX[-2:]
INFLOW = (KX.shape[0] - 2, KY.shape[0] - 2)
HAS = {
    name: [[bool((s * c[128 * k : 128 * k + 128] > 0).any()) for s in (1, -1)] for k in range(TILES)]
    for name, c in (("x", CX), ("y", CY))
}
FLOW_W = np.tile(CURRENT.T, (2, ND)).astype(f32)
GAIN = 2.0 / np.sqrt(float(ND))
STOKES_T = np.concatenate(
    [(DRIFTS.T[:, None, :] * (trig * GAIN)[None, :, None]).reshape(LEV, COMPS) for trig in (COS, SIN)]
).T.astype(f32)


def sweep_scalars():
    c = np.abs(CX.astype(np.float64)).reshape(ND, NF)
    ratio = c / (1 + c)
    cols = [1 / (1 + c), ratio] + [ratio**n for n in (2, 16, 32, 64)]
    cols += [np.zeros_like(c)] * 2
    table = np.stack(cols, -1).reshape(ND * 2, NF // 2, 8)
    return table.reshape(ND * 2, -1).astype(f32)


def fade_rows():
    rows = []
    for courant in (CX, -CX):
        part = np.maximum(courant, 0).astype(np.float64)
        rows.append(np.where(part > 0, np.log(np.maximum(part, 1e-30) / (1 + part)), -1e30))
    rows.append(1 / (1 + np.abs(CX.astype(np.float64))))
    return np.stack(rows).astype(f32)


KY = np.concatenate([KY, fade_rows()])
FADES = KY.shape[0] - 3
SWEEP = sweep_scalars()
AHEAD = (COS >= 0).astype(np.int32)


def down(x, first=None):
    top = jnp.zeros_like(x[:1]) if first is None else first
    return jnp.concatenate([top, x[:-1]], axis=0)


def up(x, last=None):
    end = jnp.zeros_like(x[:1]) if last is None else last
    return jnp.concatenate([x[1:], end], axis=0)


def hop(x, n, forward):
    z = jnp.zeros_like(x[:n])
    return jnp.concatenate([z, x[:-n]] if forward else [x[n:], z], axis=0)


def block_scan(tiles, table, base, lanes, forward):
    block = len(tiles)
    row = lambda n: table[pl.ds(base + n, 1), lanes]
    scale, ratio = row(0), row(1)
    order = list(range(block)) if forward else list(range(block - 1, -1, -1))
    out = [None] * block
    state = None
    for t in order:
        state = scale * tiles[t] if state is None else scale * tiles[t] + ratio * state
        out[t] = state
    ends = state
    ends = ends + row(block) * hop(ends, 1, forward)
    ends = ends + row(block + 1) * hop(ends, 2, forward)
    ends = ends + row(block + 2) * hop(ends, 4, forward)
    carry = hop(ends, 1, forward)
    for n, t in enumerate(order):
        out[t] = out[t] + row(n + 1) * carry
    return out


def sweep(tiles, table, k, has):
    lanes = pl.ds(128 * k, 128)
    size = len(tiles) + 3
    if has[0]:
        tiles = block_scan(tiles, table, 0, lanes, True)
    if has[1]:
        tiles = block_scan(tiles, table, size, lanes, False)
    return tiles


def source_step(spec_ref, transfer, wind, damp, sea_row, out_ref):
    spectra = spec_ref[...]
    energy = jnp.sum(spectra * spectra, axis=0, keepdims=True) * (1.0 / COMPS)
    transfer = transfer.get() if isinstance(transfer, Fetched) else transfer
    redist = jnp.dot(transfer[...], spectra.astype(jnp.bfloat16), preferred_element_type=jnp.float32)
    turns = lax.broadcasted_iota(jnp.int32, (2 * NF, NF), 0)
    turns = jnp.where(turns >= NF, turns - NF, turns)
    pick = turns == lax.broadcasted_iota(jnp.int32, (2 * NF, NF), 1)
    wind_col = jnp.sum(jnp.where(pick, wind, 0.0), axis=1, keepdims=True)
    damp_col = jnp.sum(jnp.where(pick, damp, 0.0), axis=1, keepdims=True)
    shrink = sea_row / (1.0 + 0.5 * damp_col * energy)
    first = lax.broadcasted_iota(jnp.int32, (2 * NF, 1), 0) < NF
    for pair in range(ND // 2):
        rows = slice(2 * NF * pair, 2 * NF * (pair + 1))
        near, far = (float(0.25 * (1.0 + COS[2 * pair + n])) for n in range(2))
        gain = 1.0 + jnp.where(first, near, far) * wind_col
        out_ref[rows, :] = (spectra[rows] * gain + 0.5 * redist[rows]) * shrink


def rows_source(place, spec, transfer, u, land_sea, wind, damp, out, spread, work, edges):
    u, land_sea, wind, damp, spec = (x.get() for x in (u, land_sea, wind, damp, spec))
    sea_row = land_sea[pl.ds(place[0], 1), :].astype(jnp.float32)
    turned = jnp.concatenate([u[...], u[...]], axis=0).T
    low = lax.broadcasted_iota(jnp.int32, (1, 128), 1) < LEV
    edges[pl.ds(2 * TILES, 1), :] = jnp.where(low, turned[:1], turned[127:])
    source_step(spec, transfer, wind[...], damp[...], sea_row, work)
    for k in range(TILES):
        turned = work[128 * k : 128 * k + 128, :].T
        out[k] = turned
        edges[pl.ds(k, 1), :] = turned[127:]
        edges[pl.ds(TILES + k, 1), :] = turned[:1]
    for n in range(EDGE):
        spread[pl.ds(n, NROW // 2, stride=EDGE), :] = jnp.broadcast_to(edges[pl.ds(n, 1), :], (NROW // 2, 128))


def exact(a, b):
    return jnp.dot(a, b, precision=highest, preferred_element_type=jnp.float32)


def halves(pair):
    low = lax.broadcasted_iota(jnp.int32, pair.shape, 1) < LEV
    return jnp.where(low, pair, 0.0), jnp.where(low, 0.0, pair)


def advect(mid, west, east, north, south, a, b):
    return (
        mid
        - jnp.maximum(a, 0.0) * (mid - west)
        - jnp.maximum(-a, 0.0) * (mid - east)
        - jnp.maximum(b, 0.0) * (mid - north)
        - jnp.maximum(-b, 0.0) * (mid - south)
    )


def rows_move(u, v, weights, table, spec, north, south, out, flow):
    uv = jnp.concatenate([u.get()[...], v.get()[...]], axis=0).T
    out[pl.ds(TILES, 128, stride=TILES + 1), :] = uv
    both = exact(jnp.concatenate(halves(uv), axis=0), weights.get()[...])
    for k in range(TILES):
        flow[k] = both[:, 128 * k : 128 * k + 128]
    table = table.get()
    for k in range(TILES):
        tile = lambda ref, t: ref[pl.ds(t, 8, stride=16), :]
        now, above, below = (ref.get(k) for ref in (spec, north, south))
        mids = [tile(now, t) for t in range(16)]
        moved = []
        for t in range(16):
            west = mids[t - 1] if t else down(mids[15])
            east = mids[t + 1] if t < 15 else up(mids[0])
            along, across = tile(flow.at[k], t), tile(flow.at[k], 128 + t)
            moved.append(advect(mids[t], west, east, tile(above, t), tile(below, t), along, across))
        for t, value in enumerate(sweep(moved, table, k, HAS["x"][k])):
            out[pl.ds(t * (TILES + 1) + k, 8, stride=16 * (TILES + 1)), :] = value


def senders(core, axis):
    n = lax.broadcasted_iota(jnp.int32, (NROW, NROW), axis)
    half = NROW // 2
    return jnp.where(n < half, 2 * n + core, 2 * (n - half) + 1 - core)


def columns_inflow(place, wide, table, index_west, index_east, own, other, out, flow):
    core = place[0] % 2
    pick_row = (senders(core, 1) == lax.broadcasted_iota(jnp.int32, (NROW, NROW), 0)).astype(jnp.float32)
    edge = lambda n: jnp.concatenate([ref[pl.ds(n, NROW // 2, stride=EDGE), :] for ref in (own, other)], axis=0)
    ends = exact(pick_row, edge(2 * TILES))
    flow[...] = exact(jnp.concatenate(halves(ends), axis=0), wide[...])
    behind = (place[0] * 2).astype(jnp.float32)
    added = [[], []]
    for n, (index, sign) in enumerate(((index_west, 1.0), (index_east, -1.0))):
        pick = (index[...] == senders(core, 0)).astype(jnp.float32).T
        columns = jnp.concatenate([edge(TILES * n + k) for k in range(TILES)], axis=1)
        speed = jnp.maximum(sign * flow[NROW * n : NROW * (n + 1), :], 0.0) + table[pl.ds(INFLOW[1] + n, 1), :]
        inflow = speed * exact(pick, columns)
        steps = [behind, behind + 1.0] if n == 0 else [NCOL - 1.0 - behind, NCOL - 2.0 - behind]
        for side in range(2):
            fade = table[pl.ds(FADES + 2, 1), :] * jnp.exp(table[pl.ds(FADES + n, 1), :] * steps[side])
            added[side].append(fade * inflow)
    for side in range(2):
        total = added[side][0] + added[side][1]
        for k in range(TILES):
            out[k, NROW * side : NROW * (side + 1), :] = total[:, 128 * k : 128 * k + 128]


def columns_source(
    place, land_sea, wind, damp, table, inflow, arrived, transfer, near, far, sea, turned, held, work
):
    lane = lax.broadcasted_iota(jnp.int32, (NROW, NCOL), 1)
    land = land_sea[...].astype(jnp.float32)
    for side in range(2):
        column = jnp.sum(jnp.where(lane == 2 * place[0] + side, land, 0.0), axis=1, keepdims=True)
        sea[NROW * side : NROW * (side + 1), :] = jnp.broadcast_to(column, (NROW, 128))
    for k in range(TILES):
        added = inflow.at[k]
        for side in range(2):
            places = [pl.ds(NROW * side + s, 8, stride=8) for s in range(8)]
            tiles = [
                arrived[pl.ds((2 * s + side) * (TILES + 1) + k, 8, stride=16 * (TILES + 1)), :]
                + added[places[s], :]
                for s in range(8)
            ]
            for s, value in enumerate(sweep(tiles, table, k, HAS["y"][k])):
                turned.at[k][places[s], :] = value * sea[places[s], :]
        held[128 * k : 128 * k + 128, :] = turned[k].T
    source_step(held, transfer, wind[...], damp[...], sea[...].T[:1], work)
    for k in range(TILES):
        back = work[128 * k : 128 * k + 128, :].T
        near[k] = back[:NROW]
        far[k] = back[NROW:]


def columns_flow(arrived, near, far, weights, stokes_table, east_flow, north_flow, stokes):
    uv = jnp.concatenate(
        [arrived[pl.ds(TILES + side * (TILES + 1), NROW, stride=MSG), :] for side in range(2)], axis=0
    )
    both = exact(jnp.concatenate(halves(uv), axis=0), weights[...])
    total = jnp.zeros((128, 128), jnp.float32)
    for k in range(TILES):
        east_flow[k] = both[:128, 128 * k : 128 * k + 128]
        north_flow[k] = both[128:, 128 * k : 128 * k + 128]
        spectra = jnp.concatenate([near[k], far[k]], axis=0)
        total = total + exact(spectra, stokes_table[128 * k : 128 * k + 128, :])
    stokes[...] = total


def columns_move(
    place, near, far, from_west, from_east, index_west, index_east, east_flow, north_flow, stokes, table, out,
    west_halo, east_halo, held, turned,
):
    at_end = [place[0] == 0, place[0] == NROW - 1]
    flags = [jnp.where(end, 1.0, 0.0) for end in at_end]
    across, along = (lax.broadcasted_iota(jnp.int32, (NROW, NROW), n) for n in (0, 1))
    picks = [
        (jnp.where(end, jnp.broadcast_to(index[...], (NROW, NROW)), along) == across).astype(jnp.float32).T
        for end, index in zip(at_end, (index_west, index_east))
    ]
    for k in range(TILES):
        west_halo[...] = exact(picks[0], from_west[k])
        east_halo[...] = exact(picks[1], from_east[k])
        lanes = pl.ds(128 * k, 128)
        into = [table[pl.ds(INFLOW[1] + n, 1), lanes] * flags[n] for n in range(2)]
        cells = [[ref.at[k][pl.ds(s, 8, stride=8), :] for s in range(8)] for ref in (near, far)]
        for side in range(2):
            halo = west_halo if side == 0 else east_halo
            moved = []
            for s in range(8):
                at = pl.ds(NROW * side + s, 8, stride=8)
                beyond = halo[pl.ds(s, 8, stride=8), :]
                mids = cells[side]
                north = mids[s - 1] if s else down(mids[7])
                south = mids[s + 1] if s < 7 else up(mids[0])
                west = beyond if side == 0 else cells[0][s]
                east = cells[1][s] if side == 0 else beyond
                value = advect(mids[s], west, east, north, south, east_flow.at[k][at, :], north_flow.at[k][at, :])
                moved.append(value + into[side] * beyond)
            for s, value in enumerate(sweep(moved, table, k, HAS["y"][k])):
                held[pl.ds(NROW * side + s, 8, stride=8), :] = value
        turned[128 * k : 128 * k + 128, :] = held[...].T
    half = NF // 2
    for i in range(half):
        out[pl.ds(i, 64, stride=MSG), :] = turned[pl.ds(i, 64, stride=half), :]
    for side in range(2):
        out[pl.ds(half + side, 64, stride=MSG), :] = stokes[NROW * side : NROW * (side + 1), :]


def comps_sweep(ahead, scalars, arrived, land_sea, waves, stokes, work, rows):
    half = NF // 2
    low = lax.broadcasted_iota(jnp.int32, (8, 128), 1) < NROW

    def solve(forward):
        for i in range(half):
            scale, ratio, ratio2, hop1, hop2, hop4 = (scalars[0, 8 * i + n] for n in range(6))
            tiles = [arrived[pl.ds(t * MSG + i, 8, stride=8 * MSG), :] * scale for t in range(8)]
            order = list(range(8)) if forward else list(range(7, -1, -1))
            state, states = None, {}
            for t in order:
                swapped = pltpu.roll(tiles[t], NROW, 1)
                a = tiles[t] + ratio * swapped
                b = swapped + ratio * tiles[t]
                pair = jnp.where(low, b, a) if forward else jnp.where(low, a, b)
                state = pair if state is None else pair + ratio2 * state
                states[t] = state
            ends = state
            ends = ends + hop1 * hop(ends, 1, forward)
            ends = ends + hop2 * hop(ends, 2, forward)
            ends = ends + hop4 * hop(ends, 4, forward)
            before = hop(ends, 1, forward)
            carry = before
            for t in order:
                carry = ratio2 * carry
                now = states[t] + carry
                other = tiles[t] + ratio * before
                value = jnp.where(low, other, now) if forward else jnp.where(low, now, other)
                work[pl.ds(NROW * i + t, 8, stride=8), :] = value
                before = now

    @pl.when(ahead[0] == 1)
    def _():
        solve(True)

    @pl.when(ahead[0] == 0)
    def _():
        solve(False)

    land = land_sea[...].astype(jnp.float32)
    which = lax.broadcasted_iota(jnp.int32, (128, 256), 0)
    there = lax.broadcasted_iota(jnp.int32, (128, 256), 1)
    spread = [
        (2 * jnp.where(which >= NROW, which - NROW, which) + side + jnp.where(which >= NROW, 128, 0) == there)
        .astype(jnp.float32)
        .astype(jnp.bfloat16)
        for side in range(2)
    ]
    for pair in range(half // 2):
        both = work[128 * pair : 128 * pair + 128, :].T
        total = jnp.zeros((NROW, 256), jnp.float32)
        for side in range(2):
            left = both[NROW * side : NROW * (side + 1)]
            for n in range(3):
                part = left.astype(jnp.bfloat16)
                total = total + jnp.dot(part, spread[side], preferred_element_type=jnp.float32)
                if n < 2:
                    left = left - part.astype(jnp.float32)
        for n in range(2):
            i = 2 * pair + n
            waves[NROW * i : NROW * (i + 1), :] = total[:, 128 * n : 128 * n + 128] * land
    for side in range(2):
        rows[pl.ds(side, 64, stride=2), :] = arrived[pl.ds(half + side, 64, stride=MSG), :]
    stokes[...] = rows[...].T


class Fetched:
    def __init__(self, source, buffer, sem, tiled):
        self.ref, self.tiled = buffer, tiled
        if tiled:
            parts = range(source.shape[0])
            self.copies = [pltpu.make_async_copy(source.at[k], buffer.at[k], sem.at[k]) for k in parts]
        else:
            self.copies = [pltpu.make_async_copy(source, buffer, sem.at[0])]

    def get(self, k=0):
        self.copies[k].wait()
        return self.ref.at[k] if self.tiled else self.ref


def kernel(body, outs, scratch, specs, args, flops, nbytes, limit=60):
    late = [n for n, spec in enumerate(specs) if spec in (FETCH, TILED)]

    def whole(*refs):
        size = len(refs) - 2 * len(late)
        refs, buffers, sems = list(refs[:size]), refs[size : size + len(late)], refs[size + len(late) :]
        for at, buffer, sem in zip(late, buffers, sems):
            refs[at] = Fetched(refs[at], buffer, sem, specs[at] is TILED)
        for k in range(TILES):
            for at in late:
                if k < len(refs[at].copies):
                    refs[at].copies[k].start()
        body(*refs)

    buffers = [pltpu.VMEM(args[at].shape, args[at].dtype) for at in late]
    sems = [pltpu.SemaphoreType.DMA((TILES if specs[at] is TILED else 1,)) for at in late]
    return pl.pallas_call(
        whole if late else body,
        out_shape=[jax.ShapeDtypeStruct(s, jnp.float32) for s in outs],
        in_specs=[pl.BlockSpec(memory_space=pl.ANY) if spec is TILED else spec for spec in specs],
        out_specs=[VM] * len(outs),
        scratch_shapes=[pltpu.VMEM(s, jnp.float32) for s in scratch] + buffers + sems,
        compiler_params=pltpu.CompilerParams(vmem_limit_bytes=limit << 20),
        cost_estimate=pl.CostEstimate(flops=flops, bytes_accessed=nbytes, transcendentals=0),
        interpret=INTERPRET,
    )(*args)


def step(axis, by):
    size = lax.axis_size(axis)
    return [(i, i + by) for i in range(size) if 0 <= i + by < size]


def exchange(block, per, axes=PLANE):
    sent = block.reshape(lax.axis_size(axes), per, 1, 128)
    got = lax.all_to_all(sent, axes, split_axis=0, concat_axis=0, tiled=True)
    return got.reshape(-1, 128)


def model(spectrum, land_sea, west_index, east_index, current_u, current_v, transfer, wind_rate, dissipation):
    space = lax.axis_index("space").astype(jnp.int32)
    place = space * 2 + lax.axis_index("spec").astype(jnp.int32)
    at = place.reshape(1)
    spec = spectrum.reshape(COMPS, NCOL)
    sea = land_sea[0]
    wind, damp = wind_rate.reshape(1, NF), dissipation.reshape(1, NF)
    u, v = current_u.reshape(LEV, NCOL), current_v.reshape(LEV, NCOL)
    full, flow, half, square = (COMPS, 128), (TILES, 128, 128), (TILES, NROW, 128), (128, 128)
    weights = jnp.asarray(FLOW_W)

    rows, spread = kernel(
        rows_source,
        [flow, (NROW // 2 * EDGE, 128)],
        [full, (24, 128)],
        [SM] + [FETCH] * 6,
        [at, spec, transfer, u, sea, wind, damp],
        340_000_000,
        4_000_000,
    )
    north = lax.ppermute(rows, PLANE, step(PLANE, 1))
    south = lax.ppermute(rows, PLANE, step(PLANE, -1))
    own = exchange(spread, EDGE, "space").reshape(NROW // 2, EDGE, 1, 128)
    (sent,) = kernel(
        rows_move,
        [(64 * MSG, 128)],
        [(TILES, 256, 128)],
        [FETCH, FETCH, FETCH, FETCH, TILED, TILED, TILED],
        [u, v, weights, jnp.asarray(KX), rows, north, south],
        90_000_000,
        5_000_000,
    )
    arrived = exchange(sent, MSG)

    west = lax.ppermute(own[:, :TILES], "grid", step("grid", 1))
    east = lax.ppermute(own[:, TILES : 2 * TILES], "grid", step("grid", -1))
    mine = jnp.concatenate([west, east, own[:, 2 * TILES :]], axis=1)
    other = lax.ppermute(mine, "spec", [(0, 1), (1, 0)])
    edges = [x.reshape(-1, 128) for x in (mine, other)]

    table = jnp.asarray(KY)
    (inflow,) = kernel(
        columns_inflow,
        [flow],
        [(128, COMPS)],
        [SM] + [VM] * 6,
        [at, weights, table, west_index, east_index, *edges],
        60_000_000,
        3_000_000,
        INFLOW_LIMIT,
    )
    near, far = kernel(
        columns_source,
        [half, half],
        [square, flow, full, full],
        [SM] + [VM] * 7,
        [at, sea, wind, damp, table, inflow, arrived, transfer],
        400_000_000,
        7_000_000,
        32,
    )
    a_cols, b_cols, drift = kernel(
        columns_flow,
        [flow, flow, square],
        [],
        [VM] * 5,
        [arrived, near, far, weights, jnp.asarray(STOKES_T)],
        100_000_000,
        4_000_000,
        32,
    )
    from_west = lax.ppermute(far, EVERY, step(EVERY, 1))
    from_east = lax.ppermute(near, EVERY, step(EVERY, -1))
    (sent,) = kernel(
        columns_move,
        [(64 * MSG, 128)],
        [(NROW, 128), (NROW, 128), square, full],
        [SM] + [VM] * 10,
        [at, near, far, from_west, from_east, west_index, east_index, a_cols, b_cols, drift, table],
        10_000_000,
        5_000_000,
        32,
    )
    arrived = exchange(sent, MSG)

    scalars = lax.dynamic_slice_in_dim(jnp.asarray(SWEEP), place, 1, 0)
    ahead = lax.dynamic_slice_in_dim(jnp.asarray(AHEAD), space, 1, 0)
    waves, stokes = kernel(
        comps_sweep,
        [full, square],
        [full, square],
        [SM, SM, VM, VM],
        [ahead, scalars, arrived, sea],
        100_000_000,
        2_000_000,
        32,
    )
    return waves.reshape(1, 1, NF // 2, NROW, NCOL), stokes.reshape(1, 2 * LEV, 1, NCOL)


def solution(mesh):
    rows = P("grid", None, None, PLANE, None)
    depth = P("grid", None, PLANE, None)
    return jax.shard_map(
        model,
        mesh=mesh,
        in_specs=(rows, P("grid", None, None), P("grid", None), P("grid", None), depth, depth, P(), P(), P()),
        out_specs=(P("grid", "space", "spec", None, None), depth),
        check_vma=False,
    )
```

```python
import jax
import jax.numpy as jnp
import numpy as np
from jax import lax
from jax.experimental import pallas as pl
from jax.experimental.pallas import tpu as pltpu
from jax.sharding import PartitionSpec as P


ND, NF, LEV, NCOL, NROW = 32, 36, 64, 128, 64
COMPS = ND * NF
TILES = COMPS // 128
PLANE = ("space", "spec")
EVERY = ("grid", "space", "spec")
f32 = np.float32
highest = lax.Precision.HIGHEST
INFLOW_LIMIT = 60
MSG = 20
VM = pl.BlockSpec(memory_space=pltpu.VMEM)
SM = pl.BlockSpec(memory_space=pltpu.SMEM)
FETCH = pl.BlockSpec(memory_space=pl.ANY)
TILED = object()
EDGE = 19
INTERPRET = False


def host_tables():
    steps = np.arange(NF).astype(f32)
    radian = f32(0.2199) * f32(1.1) ** steps
    wave = radian * radian / f32(9.81)
    speeds = f32(3.0) * f32(1.1) ** (-steps)
    angles = f32(2.0 * np.pi) * np.arange(ND).astype(f32) / f32(ND)
    depths = -(np.arange(LEV).astype(f32) + f32(0.5))
    decays = np.exp(2.0 * wave[:, None].astype(np.float64) * depths[None, :])
    current = decays / decays.sum(1, keepdims=True)
    drifts = (radian * wave)[:, None] * decays
    drifts = drifts / drifts.sum(0, keepdims=True)
    cosines, sines = np.cos(angles), np.sin(angles)
    return speeds, cosines, sines, current, drifts


SPEEDS, COS, SIN, CURRENT, DRIFTS = host_tables()
CX = (COS[:, None] * SPEEDS[None, :]).astype(f32).reshape(-1)
CY = (SIN[:, None] * SPEEDS[None, :]).astype(f32).reshape(-1)


def scan_table(courant, block, extra):
    rows = []
    for part in (np.maximum(courant, 0), np.maximum(-courant, 0)):
        part = part.astype(np.float64)
        ratio = part / (1.0 + part)
        rows.append(1.0 / (1.0 + part))
        rows.extend(ratio**n for n in range(1, block + 1))
        rows.extend(ratio ** (block * n) for n in extra)
    rows.append(np.maximum(courant, 0))
    rows.append(np.maximum(-courant, 0))
    return np.stack(rows).astype(f32)


KX = scan_table(CX, 16, (2, 4))
KY = scan_table(CY, 8, (2, 4))
KY[-2:] = KX[-2:]
INFLOW = (KX.shape[0] - 2, KY.shape[0] - 2)
HAS = {
    name: [[bool((s * c[128 * k : 128 * k + 128] > 0).any()) for s in (1, -1)] for k in range(TILES)]
    for name, c in (("x", CX), ("y", CY))
}
FLOW_W = np.tile(CURRENT.T, (2, ND)).astype(f32)
GAIN = 2.0 / np.sqrt(float(ND))
STOKES_T = np.concatenate(
    [(DRIFTS.T[:, None, :] * (trig * GAIN)[None, :, None]).reshape(LEV, COMPS) for trig in (COS, SIN)]
).T.astype(f32)


def sweep_scalars():
    c = np.abs(CX.astype(np.float64)).reshape(ND, NF)
    ratio = c / (1 + c)
    cols = [1 / (1 + c), ratio] + [ratio**n for n in (2, 16, 32, 64)]
    cols += [np.zeros_like(c)] * 2
    table = np.stack(cols, -1).reshape(ND * 2, NF // 2, 8)
    return table.reshape(ND * 2, -1).astype(f32)


def fade_rows():
    rows = []
    for courant in (CX, -CX):
        part = np.maximum(courant, 0).astype(np.float64)
        rows.append(np.where(part > 0, np.log(np.maximum(part, 1e-30) / (1 + part)), -1e30))
    rows.append(1 / (1 + np.abs(CX.astype(np.float64))))
    return np.stack(rows).astype(f32)


KY = np.concatenate([KY, fade_rows()])
FADES = KY.shape[0] - 3
SWEEP = sweep_scalars()
AHEAD = (COS >= 0).astype(np.int32)


def down(x, first=None):
    top = jnp.zeros_like(x[:1]) if first is None else first
    return jnp.concatenate([top, x[:-1]], axis=0)


def up(x, last=None):
    end = jnp.zeros_like(x[:1]) if last is None else last
    return jnp.concatenate([x[1:], end], axis=0)


def hop(x, n, forward):
    z = jnp.zeros_like(x[:n])
    return jnp.concatenate([z, x[:-n]] if forward else [x[n:], z], axis=0)


def block_scan(tiles, table, base, lanes, forward):
    block = len(tiles)
    row = lambda n: table[pl.ds(base + n, 1), lanes]
    scale, ratio = row(0), row(1)
    order = list(range(block)) if forward else list(range(block - 1, -1, -1))
    out = [None] * block
    state = None
    for t in order:
        state = scale * tiles[t] if state is None else scale * tiles[t] + ratio * state
        out[t] = state
    ends = state
    ends = ends + row(block) * hop(ends, 1, forward)
    ends = ends + row(block + 1) * hop(ends, 2, forward)
    ends = ends + row(block + 2) * hop(ends, 4, forward)
    carry = hop(ends, 1, forward)
    for n, t in enumerate(order):
        out[t] = out[t] + row(n + 1) * carry
    return out


def sweep(tiles, table, k, has):
    lanes = pl.ds(128 * k, 128)
    size = len(tiles) + 3
    if has[0]:
        tiles = block_scan(tiles, table, 0, lanes, True)
    if has[1]:
        tiles = block_scan(tiles, table, size, lanes, False)
    return tiles


def source_step(spec_ref, transfer, wind, damp, sea_row, out_ref):
    spectra = spec_ref[...]
    energy = jnp.sum(spectra * spectra, axis=0, keepdims=True) * (1.0 / COMPS)
    rounded = spectra.astype(jnp.bfloat16)
    product = lambda block: jnp.dot(block[...], rounded, preferred_element_type=jnp.float32)
    if isinstance(transfer, Fetched):
        redist = jnp.concatenate([product(transfer.get(k)) for k in range(TILES)], axis=0)
    else:
        redist = product(transfer)
    turns = lax.broadcasted_iota(jnp.int32, (2 * NF, NF), 0)
    turns = jnp.where(turns >= NF, turns - NF, turns)
    pick = turns == lax.broadcasted_iota(jnp.int32, (2 * NF, NF), 1)
    wind_col = jnp.sum(jnp.where(pick, wind, 0.0), axis=1, keepdims=True)
    damp_col = jnp.sum(jnp.where(pick, damp, 0.0), axis=1, keepdims=True)
    shrink = sea_row / (1.0 + 0.5 * damp_col * energy)
    first = lax.broadcasted_iota(jnp.int32, (2 * NF, 1), 0) < NF
    for pair in range(ND // 2):
        rows = slice(2 * NF * pair, 2 * NF * (pair + 1))
        near, far = (float(0.25 * (1.0 + COS[2 * pair + n])) for n in range(2))
        gain = 1.0 + jnp.where(first, near, far) * wind_col
        out_ref[rows, :] = (spectra[rows] * gain + 0.5 * redist[rows]) * shrink


def rows_source(place, spec, transfer, u, land_sea, wind, damp, out, spread, work, edges):
    u, land_sea, wind, damp, spec = (x.get() for x in (u, land_sea, wind, damp, spec))
    sea_row = land_sea[pl.ds(place[0], 1), :].astype(jnp.float32)
    turned = jnp.concatenate([u[...], u[...]], axis=0).T
    low = lax.broadcasted_iota(jnp.int32, (1, 128), 1) < LEV
    edges[pl.ds(2 * TILES, 1), :] = jnp.where(low, turned[:1], turned[127:])
    source_step(spec, transfer, wind[...], damp[...], sea_row, work)
    for k in range(TILES):
        turned = work[128 * k : 128 * k + 128, :].T
        out[k] = turned
        edges[pl.ds(k, 1), :] = turned[127:]
        edges[pl.ds(TILES + k, 1), :] = turned[:1]
    for n in range(EDGE):
        spread[pl.ds(n, NROW // 2, stride=EDGE), :] = jnp.broadcast_to(edges[pl.ds(n, 1), :], (NROW // 2, 128))


def exact(a, b):
    return jnp.dot(a, b, precision=highest, preferred_element_type=jnp.float32)


def halves(pair):
    low = lax.broadcasted_iota(jnp.int32, pair.shape, 1) < LEV
    return jnp.where(low, pair, 0.0), jnp.where(low, 0.0, pair)


def advect(mid, west, east, north, south, a, b):
    return (
        mid
        - jnp.maximum(a, 0.0) * (mid - west)
        - jnp.maximum(-a, 0.0) * (mid - east)
        - jnp.maximum(b, 0.0) * (mid - north)
        - jnp.maximum(-b, 0.0) * (mid - south)
    )


def rows_move(u, v, weights, table, spec, north, south, out, flow):
    uv = jnp.concatenate([u.get()[...], v.get()[...]], axis=0).T
    out[pl.ds(TILES, 128, stride=TILES + 1), :] = uv
    both = exact(jnp.concatenate(halves(uv), axis=0), weights.get()[...])
    for k in range(TILES):
        flow[k] = both[:, 128 * k : 128 * k + 128]
    table = table.get()
    for k in range(TILES):
        tile = lambda ref, t: ref[pl.ds(t, 8, stride=16), :]
        now, above, below = (ref.get(k) for ref in (spec, north, south))
        mids = [tile(now, t) for t in range(16)]
        moved = []
        for t in range(16):
            west = mids[t - 1] if t else down(mids[15])
            east = mids[t + 1] if t < 15 else up(mids[0])
            along, across = tile(flow.at[k], t), tile(flow.at[k], 128 + t)
            moved.append(advect(mids[t], west, east, tile(above, t), tile(below, t), along, across))
        for t, value in enumerate(sweep(moved, table, k, HAS["x"][k])):
            out[pl.ds(t * (TILES + 1) + k, 8, stride=16 * (TILES + 1)), :] = value


def senders(core, axis):
    n = lax.broadcasted_iota(jnp.int32, (NROW, NROW), axis)
    half = NROW // 2
    return jnp.where(n < half, 2 * n + core, 2 * (n - half) + 1 - core)


def columns_inflow(place, wide, table, index_west, index_east, own, other, out, flow):
    core = place[0] % 2
    pick_row = (senders(core, 1) == lax.broadcasted_iota(jnp.int32, (NROW, NROW), 0)).astype(jnp.float32)
    edge = lambda n: jnp.concatenate([ref[pl.ds(n, NROW // 2, stride=EDGE), :] for ref in (own, other)], axis=0)
    ends = exact(pick_row, edge(2 * TILES))
    flow[...] = exact(jnp.concatenate(halves(ends), axis=0), wide[...])
    behind = (place[0] * 2).astype(jnp.float32)
    added = [[], []]
    for n, (index, sign) in enumerate(((index_west, 1.0), (index_east, -1.0))):
        pick = (index[...] == senders(core, 0)).astype(jnp.float32).T
        columns = jnp.concatenate([edge(TILES * n + k) for k in range(TILES)], axis=1)
        speed = jnp.maximum(sign * flow[NROW * n : NROW * (n + 1), :], 0.0) + table[pl.ds(INFLOW[1] + n, 1), :]
        inflow = speed * exact(pick, columns)
        steps = [behind, behind + 1.0] if n == 0 else [NCOL - 1.0 - behind, NCOL - 2.0 - behind]
        for side in range(2):
            fade = table[pl.ds(FADES + 2, 1), :] * jnp.exp(table[pl.ds(FADES + n, 1), :] * steps[side])
            added[side].append(fade * inflow)
    for side in range(2):
        total = added[side][0] + added[side][1]
        for k in range(TILES):
            out[k, NROW * side : NROW * (side + 1), :] = total[:, 128 * k : 128 * k + 128]


def columns_source(
    place, land_sea, wind, damp, table, inflow, arrived, transfer, near, far, sea, turned, held, work
):
    lane = lax.broadcasted_iota(jnp.int32, (NROW, NCOL), 1)
    land = land_sea[...].astype(jnp.float32)
    for side in range(2):
        column = jnp.sum(jnp.where(lane == 2 * place[0] + side, land, 0.0), axis=1, keepdims=True)
        sea[NROW * side : NROW * (side + 1), :] = jnp.broadcast_to(column, (NROW, 128))
    for k in range(TILES):
        added = inflow.at[k]
        for side in range(2):
            places = [pl.ds(NROW * side + s, 8, stride=8) for s in range(8)]
            tiles = [
                arrived[pl.ds((2 * s + side) * (TILES + 1) + k, 8, stride=16 * (TILES + 1)), :]
                + added[places[s], :]
                for s in range(8)
            ]
            for s, value in enumerate(sweep(tiles, table, k, HAS["y"][k])):
                turned.at[k][places[s], :] = value * sea[places[s], :]
        held[128 * k : 128 * k + 128, :] = turned[k].T
    source_step(held, transfer, wind[...], damp[...], sea[...].T[:1], work)
    for k in range(TILES):
        back = work[128 * k : 128 * k + 128, :].T
        near[k] = back[:NROW]
        far[k] = back[NROW:]


def columns_flow(arrived, near, far, weights, stokes_table, east_flow, north_flow, stokes):
    uv = jnp.concatenate(
        [arrived[pl.ds(TILES + side * (TILES + 1), NROW, stride=MSG), :] for side in range(2)], axis=0
    )
    both = exact(jnp.concatenate(halves(uv), axis=0), weights[...])
    total = jnp.zeros((128, 128), jnp.float32)
    for k in range(TILES):
        east_flow[k] = both[:128, 128 * k : 128 * k + 128]
        north_flow[k] = both[128:, 128 * k : 128 * k + 128]
        spectra = jnp.concatenate([near[k], far[k]], axis=0)
        total = total + exact(spectra, stokes_table[128 * k : 128 * k + 128, :])
    stokes[...] = total


def columns_move(
    place, near, far, from_west, from_east, index_west, index_east, east_flow, north_flow, stokes, table, out,
    west_halo, east_halo, held, turned,
):
    at_end = [place[0] == 0, place[0] == NROW - 1]
    flags = [jnp.where(end, 1.0, 0.0) for end in at_end]
    across, along = (lax.broadcasted_iota(jnp.int32, (NROW, NROW), n) for n in (0, 1))
    picks = [
        (jnp.where(end, jnp.broadcast_to(index[...], (NROW, NROW)), along) == across).astype(jnp.float32).T
        for end, index in zip(at_end, (index_west, index_east))
    ]
    halos = [
        exact(pick, jnp.concatenate([source[k] for k in range(TILES)], axis=1))
        for pick, source in zip(picks, (from_west, from_east))
    ]
    for k in range(TILES):
        west_halo[k] = halos[0][:, 128 * k : 128 * k + 128]
        east_halo[k] = halos[1][:, 128 * k : 128 * k + 128]
    for k in range(TILES):
        lanes = pl.ds(128 * k, 128)
        into = [table[pl.ds(INFLOW[1] + n, 1), lanes] * flags[n] for n in range(2)]
        cells = [[ref.at[k][pl.ds(s, 8, stride=8), :] for s in range(8)] for ref in (near, far)]
        for side in range(2):
            halo = west_halo if side == 0 else east_halo
            moved = []
            for s in range(8):
                at = pl.ds(NROW * side + s, 8, stride=8)
                beyond = halo.at[k][pl.ds(s, 8, stride=8), :]
                mids = cells[side]
                north = mids[s - 1] if s else down(mids[7])
                south = mids[s + 1] if s < 7 else up(mids[0])
                west = beyond if side == 0 else cells[0][s]
                east = cells[1][s] if side == 0 else beyond
                value = advect(mids[s], west, east, north, south, east_flow.at[k][at, :], north_flow.at[k][at, :])
                moved.append(value + into[side] * beyond)
            for s, value in enumerate(sweep(moved, table, k, HAS["y"][k])):
                held[pl.ds(NROW * side + s, 8, stride=8), :] = value
        turned[128 * k : 128 * k + 128, :] = held[...].T
    half = NF // 2
    for i in range(half):
        out[pl.ds(i, 64, stride=MSG), :] = turned[pl.ds(i, 64, stride=half), :]
    for side in range(2):
        out[pl.ds(half + side, 64, stride=MSG), :] = stokes[NROW * side : NROW * (side + 1), :]


def comps_sweep(ahead, scalars, arrived, land_sea, waves, stokes, work, rows):
    half = NF // 2
    low = lax.broadcasted_iota(jnp.int32, (8, 128), 1) < NROW

    def solve(forward):
        for i in range(half):
            scale, ratio, ratio2, hop1, hop2, hop4 = (scalars[0, 8 * i + n] for n in range(6))
            tiles = [arrived[pl.ds(t * MSG + i, 8, stride=8 * MSG), :] * scale for t in range(8)]
            order = list(range(8)) if forward else list(range(7, -1, -1))
            state, states = None, {}
            for t in order:
                swapped = pltpu.roll(tiles[t], NROW, 1)
                a = tiles[t] + ratio * swapped
                b = swapped + ratio * tiles[t]
                pair = jnp.where(low, b, a) if forward else jnp.where(low, a, b)
                state = pair if state is None else pair + ratio2 * state
                states[t] = state
            ends = state
            ends = ends + hop1 * hop(ends, 1, forward)
            ends = ends + hop2 * hop(ends, 2, forward)
            ends = ends + hop4 * hop(ends, 4, forward)
            before = hop(ends, 1, forward)
            carry = before
            for t in order:
                carry = ratio2 * carry
                now = states[t] + carry
                other = tiles[t] + ratio * before
                value = jnp.where(low, other, now) if forward else jnp.where(low, now, other)
                work[pl.ds(NROW * i + t, 8, stride=8), :] = value
                before = now

    @pl.when(ahead[0] == 1)
    def _():
        solve(True)

    @pl.when(ahead[0] == 0)
    def _():
        solve(False)

    land = land_sea[...].astype(jnp.float32)
    which = lax.broadcasted_iota(jnp.int32, (128, 256), 0)
    there = lax.broadcasted_iota(jnp.int32, (128, 256), 1)
    spread = [
        (2 * jnp.where(which >= NROW, which - NROW, which) + side + jnp.where(which >= NROW, 128, 0) == there)
        .astype(jnp.float32)
        .astype(jnp.bfloat16)
        for side in range(2)
    ]
    for pair in range(half // 2):
        both = work[128 * pair : 128 * pair + 128, :].T
        total = jnp.zeros((NROW, 256), jnp.float32)
        for side in range(2):
            left = both[NROW * side : NROW * (side + 1)]
            for n in range(2):
                part = left.astype(jnp.bfloat16)
                total = total + jnp.dot(part, spread[side], preferred_element_type=jnp.float32)
                if n == 0:
                    left = left - part.astype(jnp.float32)
        for n in range(2):
            i = 2 * pair + n
            waves[NROW * i : NROW * (i + 1), :] = total[:, 128 * n : 128 * n + 128] * land
    for side in range(2):
        rows[pl.ds(side, 64, stride=2), :] = arrived[pl.ds(half + side, 64, stride=MSG), :]
    stokes[...] = rows[...].T


class Fetched:
    def __init__(self, source, buffer, sem, tiled):
        self.ref, self.tiled = buffer, tiled
        if tiled:
            parts = range(source.shape[0])
            self.copies = [pltpu.make_async_copy(source.at[k], buffer.at[k], sem.at[k]) for k in parts]
        else:
            self.copies = [pltpu.make_async_copy(source, buffer, sem.at[0])]

    def get(self, k=0):
        self.copies[k].wait()
        return self.ref.at[k] if self.tiled else self.ref


def kernel(body, outs, scratch, specs, args, flops, nbytes, limit=60):
    late = [n for n, spec in enumerate(specs) if spec in (FETCH, TILED)]

    def whole(*refs):
        size = len(refs) - 2 * len(late)
        refs, buffers, sems = list(refs[:size]), refs[size : size + len(late)], refs[size + len(late) :]
        for at, buffer, sem in zip(late, buffers, sems):
            refs[at] = Fetched(refs[at], buffer, sem, specs[at] is TILED)
        for k in range(TILES):
            for at in late:
                if k < len(refs[at].copies):
                    refs[at].copies[k].start()
        body(*refs)

    buffers = [pltpu.VMEM(args[at].shape, args[at].dtype) for at in late]
    sems = [pltpu.SemaphoreType.DMA((TILES if specs[at] is TILED else 1,)) for at in late]
    return pl.pallas_call(
        whole if late else body,
        out_shape=[jax.ShapeDtypeStruct(s, jnp.float32) for s in outs],
        in_specs=[pl.BlockSpec(memory_space=pl.ANY) if spec is TILED else spec for spec in specs],
        out_specs=[VM] * len(outs),
        scratch_shapes=[pltpu.VMEM(s, jnp.float32) for s in scratch] + buffers + sems,
        compiler_params=pltpu.CompilerParams(vmem_limit_bytes=limit << 20),
        cost_estimate=pl.CostEstimate(flops=flops, bytes_accessed=nbytes, transcendentals=0),
        interpret=INTERPRET,
    )(*args)


def step(axis, by):
    size = lax.axis_size(axis)
    return [(i, i + by) for i in range(size) if 0 <= i + by < size]


def exchange(block, per, axes=PLANE):
    sent = block.reshape(lax.axis_size(axes), per, 1, 128)
    got = lax.all_to_all(sent, axes, split_axis=0, concat_axis=0, tiled=True)
    return got.reshape(-1, 128)


def model(spectrum, land_sea, west_index, east_index, current_u, current_v, transfer, wind_rate, dissipation):
    space = lax.axis_index("space").astype(jnp.int32)
    place = space * 2 + lax.axis_index("spec").astype(jnp.int32)
    at = place.reshape(1)
    spec = spectrum.reshape(COMPS, NCOL)
    sea = land_sea[0]
    wind, damp = wind_rate.reshape(1, NF), dissipation.reshape(1, NF)
    u, v = current_u.reshape(LEV, NCOL), current_v.reshape(LEV, NCOL)
    full, flow, half, square = (COMPS, 128), (TILES, 128, 128), (TILES, NROW, 128), (128, 128)
    weights = jnp.asarray(FLOW_W)

    rows, spread = kernel(
        rows_source,
        [flow, (NROW // 2 * EDGE, 128)],
        [full, (24, 128)],
        [SM, FETCH, TILED] + [FETCH] * 4,
        [at, spec, transfer.reshape(TILES, 128, COMPS), u, sea, wind, damp],
        340_000_000,
        4_000_000,
    )
    north = lax.ppermute(rows, PLANE, step(PLANE, 1))
    south = lax.ppermute(rows, PLANE, step(PLANE, -1))
    own = exchange(spread, EDGE, "space").reshape(NROW // 2, EDGE, 1, 128)
    (sent,) = kernel(
        rows_move,
        [(64 * MSG, 128)],
        [(TILES, 256, 128)],
        [FETCH, FETCH, FETCH, FETCH, TILED, TILED, TILED],
        [u, v, weights, jnp.asarray(KX), rows, north, south],
        90_000_000,
        5_000_000,
    )
    arrived = exchange(sent, MSG)

    west = lax.ppermute(own[:, :TILES], "grid", step("grid", 1))
    east = lax.ppermute(own[:, TILES : 2 * TILES], "grid", step("grid", -1))
    mine = jnp.concatenate([west, east, own[:, 2 * TILES :]], axis=1)
    other = lax.ppermute(mine, "spec", [(0, 1), (1, 0)])
    edges = [x.reshape(-1, 128) for x in (mine, other)]

    table = jnp.asarray(KY)
    (inflow,) = kernel(
        columns_inflow,
        [flow],
        [(128, COMPS)],
        [SM] + [VM] * 6,
        [at, weights, table, west_index, east_index, *edges],
        60_000_000,
        3_000_000,
        INFLOW_LIMIT,
    )
    near, far = kernel(
        columns_source,
        [half, half],
        [square, flow, full, full],
        [SM] + [VM] * 7,
        [at, sea, wind, damp, table, inflow, arrived, transfer],
        400_000_000,
        7_000_000,
        32,
    )
    a_cols, b_cols, drift = kernel(
        columns_flow,
        [flow, flow, square],
        [],
        [VM] * 5,
        [arrived, near, far, weights, jnp.asarray(STOKES_T)],
        100_000_000,
        4_000_000,
        32,
    )
    from_west = lax.ppermute(far, EVERY, step(EVERY, 1))
    from_east = lax.ppermute(near, EVERY, step(EVERY, -1))
    (sent,) = kernel(
        columns_move,
        [(64 * MSG, 128)],
        [half, half, square, full],
        [SM] + [VM] * 10,
        [at, near, far, from_west, from_east, west_index, east_index, a_cols, b_cols, drift, table],
        10_000_000,
        5_000_000,
        32,
    )
    arrived = exchange(sent, MSG)

    scalars = lax.dynamic_slice_in_dim(jnp.asarray(SWEEP), place, 1, 0)
    ahead = lax.dynamic_slice_in_dim(jnp.asarray(AHEAD), space, 1, 0)
    waves, stokes = kernel(
        comps_sweep,
        [full, square],
        [full, square],
        [SM, SM, VM, VM],
        [ahead, scalars, arrived, sea],
        100_000_000,
        2_000_000,
        32,
    )
    return waves.reshape(1, 1, NF // 2, NROW, NCOL), stokes.reshape(1, 2 * LEV, 1, NCOL)


def solution(mesh):
    rows = P("grid", None, None, PLANE, None)
    depth = P("grid", None, PLANE, None)
    return jax.shard_map(
        model,
        mesh=mesh,
        in_specs=(rows, P("grid", None, None), P("grid", None), P("grid", None), depth, depth, P(), P(), P()),
        out_specs=(P("grid", "space", "spec", None, None), depth),
        check_vma=False,
    )
```
